256 devices in a mesh: wide: 32 (over z, x_lo, core), req: 8 (over y, x_hi).
Axes of the slice: x: 4 (x_hi: 2, x_lo: 2; x = x_hi * 2 + x_lo), y: 4, z: 8, core: 2. Of those that a mesh axis runs over, the one named last changes fastest.
Arguments:
- x_in: bfloat16 [2048, 8192], P('req', 'wide'), may hold values from -6 to 6
- w_xz: bfloat16 [8192, 2, 16384], P('req', None, 'wide'), may hold values from -0.0625 to 0.0625
- w_dt: bfloat16 [8192, 256], P('req', 'wide'), may hold values from -0.0625 to 0.0625
- w_bc: bfloat16 [8192, 4096], P('req', 'wide'), may hold values from -0.0625 to 0.0625
- dt_bias: float32 [256], P('wide'), may hold values from -7 to -3
- a_log: float32 [256], P('wide'), may hold values from 0 to 2.77
- d_skip: float32 [256], P('wide'), may hold values from 0.5 to 1.5
- conv_x_w: float32 [4, 16384], P(None, 'wide'), may hold values from -3 to 3
- conv_x_b: float32 [16384], P('wide'), may hold values from -3 to 3
- conv_bc_w: float32 [4, 4096], P(None, 'wide'), may hold values from -3 to 3
- conv_bc_b: float32 [4096], P('wide'), may hold values from -3 to 3
- norm_gain: float32 [16384], P('wide'), may hold values from 0.5 to 1.5
- stretch_start: int32 [8, 2], P('req'), may hold values from 0 to 255, as said below
- prefix_len: int32 [16], P('req'), may hold values from 0 to 32768, as said below
- state_slot: int32 [16], replicated, may hold values from 0 to 63, as said below
- ssm_pool: float32 [64, 256, 64, 256], P('req', 'wide'), may hold values from -6 to 6
- conv_x_pool: bfloat16 [64, 3, 16384], P('req', None, 'wide'), may hold values from -6 to 6
- conv_bc_pool: bfloat16 [64, 3, 4096], P('req', None, 'wide'), may hold values from -6 to 6
Outputs:
- y_out: bfloat16 [2048, 16384], P('req', 'wide')
- new_state: float32 [16, 256, 64, 256], P('req', 'wide')
The draws below stay inside these ranges and needn't reach their ends.
Inputs may be any that keep to these rules, and one draw needn't show every extreme that they name: `stretch_start`: each row is 0 first and rises strictly; the 2 requests of an index of req cover its 256 tokens in order. `prefix_len`: zero means no cached state; in every draw some request has zero and one has 32768. `state_slot`: distinct slots; slot s is owned by index s // 8 of req; owners hold very uneven numbers of the requested slots.
All inputs are finite; a program needn't handle non-finite values.
Results may differ from the reference program's by a relative error of at most 0.014.
Values may be sent and summed in bfloat16 or wider, within the bound.
A program may use at most 128 MiB of HBM per device.

```python
import jax
import jax.numpy as jnp
from jax import lax

D = 8192
HEADS = 256
HEAD_DIM = 64
STATE = 256
GROUPS = 8
CONV = 4
TOK_G = 256
REQ_G = 2
SLOTS_DEV = 8
PREFIX_MOST = 32768
TOKENS = 2048
REQS = 16
STATE_SLOT_TOTAL = 64
N_REQ = 8


def draw_stretch_start(key, part):
    row_keys = jax.random.split(key, N_REQ)

    def one_row(row_key):
        split_positions = jax.random.permutation(row_key, TOK_G - 1)[:REQ_G - 1] + 1
        return jnp.concatenate([jnp.zeros((1,), jnp.int32), jnp.sort(split_positions).astype(jnp.int32)])
    rows = jax.vmap(one_row)(row_keys).astype(jnp.int32)
    first_key = jax.random.fold_in(key, 7)
    first_picks = jax.random.permutation(first_key, TOK_G - 2)[:REQ_G - 2] + 1
    first_row = jnp.concatenate([jnp.zeros((1,), jnp.int32), jnp.sort(first_picks).astype(jnp.int32), jnp.full((1,), TOK_G - 1, jnp.int32)])
    rows = rows.at[0].set(first_row)
    return rows.astype(jnp.int32)


def draw_prefix_len(key, part):
    initial_random_key, second_key = jax.random.split(key)
    values = jax.random.randint(initial_random_key, (REQS,), -(PREFIX_MOST // 4), PREFIX_MOST + 1)
    values = jnp.maximum(values, 0)
    selected_entries = jax.random.permutation(second_key, REQS)
    values = values.at[selected_entries[0]].set(0)
    if REQS > 1:
        values = values.at[selected_entries[1]].set(PREFIX_MOST)
    return values.astype(jnp.int32)


def draw_state_slot(key, part):
    initial_random_key, second_key, third_key = jax.random.split(key, 3)
    holder_preference = jax.random.randint(initial_random_key, (N_REQ,), 0, 4)
    random_jitter = jax.random.randint(second_key, (STATE_SLOT_TOTAL,), 0, 4096)
    holder_numbers = jnp.arange(STATE_SLOT_TOTAL, dtype=jnp.int32) // SLOTS_DEV
    combined_scores = (holder_preference[holder_numbers] * 4096 + random_jitter) * STATE_SLOT_TOTAL + jnp.arange(STATE_SLOT_TOTAL, dtype=jnp.int32)
    combined_scores = combined_scores.at[STATE_SLOT_TOTAL - 1].set(jnp.max(combined_scores) + 1)
    top_values, chosen = lax.top_k(combined_scores, REQS)
    shuffle = jax.random.permutation(third_key, REQS)
    return chosen[shuffle].astype(jnp.int32)


def block_levels(stream_key, shape, cuts, least, largest):
    loudness, own = 1.0, jax.random.fold_in(stream_key, 6)
    for dim, blocks in cuts:
        heights = jnp.exp(jax.random.uniform(jax.random.fold_in(own, dim), (blocks,), jnp.float32, least / len(cuts), largest / len(cuts)))
        loudness = loudness * jnp.repeat(heights, shape[dim] // blocks).reshape([-1 if axis == dim else 1 for axis in range(len(shape))])
    return loudness


def scatter_about(rng, shape, spread, bound, cuts=(), kind=jnp.bfloat16):
    array = spread * jax.random.normal(rng, shape, jnp.float32)
    if cuts:
        array = array * block_levels(rng, shape, cuts, -0.22, 0.18)
    return jnp.clip(array, -bound, bound).astype(kind)


def setup_inputs(seed: int = 0) -> dict:
    key_list = jax.random.split(jax.random.key(seed), 19)
    x_in = scatter_about(key_list[0], (TOKENS, D), 1.0, 6.0, ((0, 8), (1, 32)))
    w_xz = scatter_about(key_list[1], (D, 2, HEADS * HEAD_DIM), D ** -0.5, 0.0625, ((0, 8), (2, 32)))
    w_dt = scatter_about(key_list[2], (D, HEADS), D ** -0.5, 0.0625, ((0, 8), (1, 32)))
    w_bc = scatter_about(key_list[3], (D, 2 * GROUPS * STATE), D ** -0.5, 0.0625, ((0, 8), (1, 32)))
    dt_bias = jnp.clip(-7.0 + 4.0 * jax.random.uniform(key_list[4], (HEADS,), jnp.float32) ** block_levels(key_list[4], (HEADS,), ((0, 32),), -0.2, 0.2), -7.0, -3.0)
    a_log = jnp.clip(2.77 * jax.random.uniform(key_list[5], (HEADS,), jnp.float32) ** block_levels(key_list[5], (HEADS,), ((0, 32),), -0.2, 0.2), 0.0, 2.77)
    d_skip = jnp.clip(0.5 + 1.0 * jax.random.uniform(key_list[6], (HEADS,), jnp.float32) ** block_levels(key_list[6], (HEADS,), ((0, 32),), -0.2, 0.2), 0.5, 1.5)
    conv_x_w = scatter_about(key_list[7], (CONV, HEADS * HEAD_DIM), 0.5, 3.0, ((1, 32),), jnp.float32)
    conv_x_b = scatter_about(key_list[8], (HEADS * HEAD_DIM,), 0.5, 3.0, ((0, 32),), jnp.float32)
    conv_bc_w = scatter_about(key_list[9], (CONV, 2 * GROUPS * STATE), 0.5, 3.0, ((1, 32),), jnp.float32)
    conv_bc_b = scatter_about(key_list[10], (2 * GROUPS * STATE,), 0.5, 3.0, ((0, 32),), jnp.float32)
    norm_gain = jnp.clip(1.0 + 0.1 * jax.random.normal(key_list[11], (HEADS * HEAD_DIM,), jnp.float32), 0.5, 1.5)
    stretch_start = draw_stretch_start(jax.random.fold_in(key_list[18], 71), 0)
    prefix_len = draw_prefix_len(jax.random.fold_in(key_list[18], 71), 0)
    state_slot = draw_state_slot(jax.random.fold_in(key_list[18], 71), 0)
    ssm_pool = scatter_about(key_list[15], (STATE_SLOT_TOTAL, HEADS, HEAD_DIM, STATE), 1.0, 6.0, ((0, 8), (1, 32)), jnp.float32)
    conv_x_pool = scatter_about(key_list[16], (STATE_SLOT_TOTAL, CONV - 1, HEADS * HEAD_DIM), 1.0, 6.0, ((0, 8), (2, 32)))
    conv_bc_pool = scatter_about(key_list[17], (STATE_SLOT_TOTAL, CONV - 1, 2 * GROUPS * STATE), 1.0, 6.0, ((0, 8), (2, 32)))
    return {"x_in": x_in, "w_xz": w_xz, "w_dt": w_dt, "w_bc": w_bc, "dt_bias": dt_bias, "a_log": a_log, "d_skip": d_skip, "conv_x_w": conv_x_w, "conv_x_b": conv_x_b, "conv_bc_w": conv_bc_w, "conv_bc_b": conv_bc_b, "norm_gain": norm_gain, "stretch_start": stretch_start, "prefix_len": prefix_len, "state_slot": state_slot, "ssm_pool": ssm_pool, "conv_x_pool": conv_x_pool, "conv_bc_pool": conv_bc_pool}


NORM_EPS = 1e-05

def segments(starts, count_tok):
    position = jnp.arange(count_tok, dtype=jnp.int32)
    seg_ids = lax.optimization_barrier(jnp.sum((position[:, None] >= starts[None, :]).astype(jnp.int32), 1)) - 1
    member = seg_ids[:, None] == jnp.arange(starts.shape[0], dtype=jnp.int32)[None, :]
    offset = position - lax.optimization_barrier(jnp.sum(jnp.where(member, starts[None, :], 0), 1))
    same_req = seg_ids[:, None] == seg_ids[None, :]
    causal = position[:, None] >= position[None, :]
    return (member.astype(jnp.float32), offset, (same_req & causal).astype(jnp.float32))

def causal_conv(inputs, cache, kernel, bias, member, offset):
    kernel_len = kernel.shape[0]
    count_tok, channels = inputs.shape
    count_req = cache.shape[0]
    history = jnp.dot(member, cache.reshape(count_req, (kernel_len - 1) * channels), precision=lax.Precision.HIGHEST)
    history = history.reshape(count_tok, kernel_len - 1, channels)
    values = inputs.astype(jnp.float32)
    total = bias[None, :] + kernel[kernel_len - 1][None, :] * values
    for lag_step in range(1, kernel_len):
        shifted = jnp.concatenate([jnp.zeros((lag_step, channels), jnp.float32), values[:count_tok - lag_step]], 0)
        earlier = jnp.zeros((count_tok, channels), jnp.float32)
        for slot_place in range(kernel_len - 1):
            hit_place = offset - lag_step + kernel_len - 1 == slot_place
            earlier = earlier + jnp.where(hit_place[:, None], history[:, slot_place], 0.0)
        chosen = jnp.where((offset >= lag_step)[:, None], shifted, earlier)
        total = total + kernel[kernel_len - 1 - lag_step][None, :] * chosen
    return jax.nn.silu(total).astype(jnp.bfloat16)

def mixer(inputs, dt_raw, b_maps, c_maps, start_state, member, mask, dt_bias, a_log, d_skip):
    count_tok, heads_here, head_width = inputs.shape
    groups_here = b_maps.shape[1]
    per_group = heads_here // groups_here
    count_req = start_state.shape[0]
    state_width = b_maps.shape[2]
    high = lax.Precision.HIGHEST
    step_size = jax.nn.softplus(dt_raw.astype(jnp.float32) + dt_bias[None, :])
    decay_rate = step_size * (-jnp.exp(a_log))[None, :]
    cumulative = jnp.dot(mask, decay_rate, precision=high)
    scores = jnp.einsum('tgn,sgn->gts', c_maps.astype(jnp.float32), b_maps.astype(jnp.float32), precision=high)
    spread_gap = jnp.minimum(cumulative.T[:, :, None] - cumulative.T[:, None, :], 0.0)
    decay = jnp.exp(spread_gap) * mask[None] * step_size.T[:, None, :]
    weights = decay.reshape(groups_here, per_group, count_tok, count_tok) * scores[:, None]
    weights = weights.astype(jnp.bfloat16).reshape(heads_here, count_tok, count_tok)
    values = inputs.astype(jnp.float32)
    intra = jnp.einsum('hts,shp->thp', weights.astype(jnp.float32), values, precision=high)
    grouped_state = start_state.reshape(count_req, groups_here, per_group, head_width, state_width)
    from_state = jnp.einsum('tgn,jgkpn->jtgkp', c_maps.astype(jnp.float32), grouped_state, precision=high)
    from_state = jnp.einsum('tj,jtgkp->tgkp', member, from_state, precision=high).reshape(count_tok, heads_here, head_width)
    from_state = from_state * jnp.exp(cumulative)[:, :, None]
    result = intra + from_state + d_skip[None, :, None] * values
    ends = jnp.dot(member.T, decay_rate, precision=high)
    to_end = jnp.exp(jnp.dot(member, ends, precision=high) - cumulative)
    carried = (to_end * step_size)[:, :, None] * values
    split_req = (member.T[:, :, None, None] * carried[None]).astype(jnp.bfloat16)
    split_req = split_req.reshape(count_req, count_tok, groups_here, per_group, head_width)
    fresh = jnp.einsum('jtgkp,tgn->jgkpn', split_req.astype(jnp.float32), b_maps.astype(jnp.float32), precision=high)
    fresh = fresh.reshape(count_req, heads_here, head_width, state_width)
    final_state = jnp.exp(ends)[:, :, None, None] * start_state + fresh
    return (result, final_state)

def reference(x_in, w_xz, w_dt, w_bc, dt_bias, a_log, d_skip, conv_x_w, conv_x_b, conv_bc_w, conv_bc_b, norm_gain, stretch_start, prefix_len, state_slot, ssm_pool, conv_x_pool, conv_bc_pool):
    channels = HEADS * HEAD_DIM
    flat_xz = w_xz.reshape(D, 2 * channels)
    grouped_x = x_in.reshape(N_REQ, TOK_G, D)
    slot_rows = state_slot.reshape(N_REQ, REQ_G)
    prefix_rows = prefix_len.reshape(N_REQ, REQ_G)

    def one_group(items):
        features, starts, prefix_here, slot_here = items
        proj_xz = jnp.dot(features, flat_xz, preferred_element_type=jnp.float32).astype(jnp.bfloat16)
        proj_xz = proj_xz.reshape(TOK_G, 2, channels)
        dt_raw = jnp.dot(features, w_dt, preferred_element_type=jnp.float32).astype(jnp.bfloat16)
        bc_raw = jnp.dot(features, w_bc, preferred_element_type=jnp.float32).astype(jnp.bfloat16)
        member, offset, mask = segments(starts, TOK_G)
        has_cache = (prefix_here > 0).astype(jnp.float32)
        start_state = ssm_pool[slot_here] * has_cache[:, None, None, None]
        cache_x = conv_x_pool[slot_here].astype(jnp.float32) * has_cache[:, None, None]
        cache_bc = conv_bc_pool[slot_here].astype(jnp.float32) * has_cache[:, None, None]
        x_conv = causal_conv(proj_xz[:, 1], cache_x, conv_x_w, conv_x_b, member, offset)
        bc_conv = causal_conv(bc_raw, cache_bc, conv_bc_w, conv_bc_b, member, offset)
        bc_conv = bc_conv.reshape(TOK_G, GROUPS, 2, STATE)
        result, final_state = mixer(x_conv.reshape(TOK_G, HEADS, HEAD_DIM), dt_raw, bc_conv[:, :, 0], bc_conv[:, :, 1], start_state, member, mask, dt_bias, a_log, d_skip)
        gated = result.reshape(TOK_G, channels) * jax.nn.silu(proj_xz[:, 0].astype(jnp.float32))
        by_group = gated.reshape(TOK_G, GROUPS, channels // GROUPS)
        mean_sq = lax.optimization_barrier(jnp.mean(by_group * by_group, -1, keepdims=True))
        normed = (by_group * lax.rsqrt(mean_sq + NORM_EPS)).reshape(TOK_G, channels) * norm_gain[None, :]
        return (normed.astype(jnp.bfloat16), final_state)
    outputs, states = lax.map(one_group, (grouped_x, stretch_start, prefix_rows, slot_rows))
    return (outputs.reshape(TOKENS, channels), states.reshape(REQS, HEADS, HEAD_DIM, STATE))
```

```python
import functools

import jax
import jax.numpy as jnp
from jax import lax
from jax.experimental import pallas as pl
from jax.experimental.pallas import tpu as pltpu
from jax.sharding import PartitionSpec as P

HEADS = 256
HEAD_DIM = 64
GROUPS = 8
NORM_EPS = 1e-05
MESH = pl.DeviceIdType.MESH
BF = jnp.bfloat16
F32 = jnp.float32


def partner_2(block, axis, bit):
    count = lax.axis_size(axis)
    route = []
    for low in range(count):
        high = low | 1 << bit
        if high != low and high < count:
            route += [(low, high), (high, low)]
    return lax.ppermute(block, axis, route)


def segments(starts, count_tok):
    position = jnp.arange(count_tok, dtype=jnp.int32)
    seg_ids = jnp.sum((position[:, None] >= starts[None, :]).astype(jnp.int32), 1) - 1
    member = seg_ids[:, None] == jnp.arange(starts.shape[0], dtype=jnp.int32)[None, :]
    offset = position - jnp.sum(jnp.where(member, starts[None, :], 0), 1)
    same_req = seg_ids[:, None] == seg_ids[None, :]
    causal = position[:, None] >= position[None, :]
    return (member.astype(jnp.float32), offset, (same_req & causal).astype(jnp.float32))


def causal_conv(inputs, cache, kernel, bias, member, offset):
    kernel_len = kernel.shape[0]
    count_tok, channels = inputs.shape
    count_req = cache.shape[0]
    history = jnp.dot(
        member,
        cache.reshape(count_req, (kernel_len - 1) * channels),
        precision=lax.Precision.HIGHEST,
    )
    history = history.reshape(count_tok, kernel_len - 1, channels)
    values = inputs.astype(jnp.float32)
    total = bias[None, :] + kernel[kernel_len - 1][None, :] * values
    for lag_step in range(1, kernel_len):
        shifted = jnp.concatenate(
            [jnp.zeros((lag_step, channels), jnp.float32), values[: count_tok - lag_step]], 0
        )
        earlier = jnp.zeros((count_tok, channels), jnp.float32)
        for slot_place in range(kernel_len - 1):
            hit_place = offset - lag_step + kernel_len - 1 == slot_place
            earlier = earlier + jnp.where(hit_place[:, None], history[:, slot_place], 0.0)
        chosen = jnp.where((offset >= lag_step)[:, None], shifted, earlier)
        total = total + kernel[kernel_len - 1 - lag_step][None, :] * chosen
    return jax.nn.silu(total).astype(jnp.bfloat16)


def mixer(inputs, dt_raw, b_maps, c_maps, start_state, member, mask, dt_bias, a_log, d_skip):
    high = lax.Precision.HIGHEST
    step_size = jax.nn.softplus(dt_raw.astype(jnp.float32) + dt_bias[None, :])
    decay_rate = step_size * (-jnp.exp(a_log))[None, :]
    cumulative = jnp.dot(mask, decay_rate, precision=high)
    scores = jnp.dot(c_maps, b_maps.T, preferred_element_type=jnp.float32)
    spread_gap = jnp.minimum(cumulative.T[:, :, None] - cumulative.T[:, None, :], 0.0)
    decay = jnp.exp(spread_gap) * mask[None] * step_size.T[:, None, :]
    weights = (decay * scores[None]).astype(jnp.bfloat16)
    intra = jnp.einsum("hts,shp->thp", weights, inputs, preferred_element_type=jnp.float32)
    values = inputs.astype(jnp.float32)
    from_state = jnp.einsum(
        "tn,jhpn->jthp", c_maps.astype(jnp.float32), start_state, precision=high
    )
    from_state = jnp.einsum("tj,jthp->thp", member, from_state, precision=high)
    from_state = from_state * jnp.exp(cumulative)[:, :, None]
    result = intra + from_state + d_skip[None, :, None] * values
    ends = jnp.dot(member.T, decay_rate, precision=high)
    to_end = jnp.exp(jnp.dot(member, ends, precision=high) - cumulative)
    carried = (to_end * step_size)[:, :, None] * values
    split_req = (member.T[:, :, None, None] * carried[None]).astype(jnp.bfloat16)
    fresh = jnp.einsum("jthp,tn->jhpn", split_req, b_maps, preferred_element_type=jnp.float32)
    final_state = jnp.exp(ends)[:, :, None, None] * start_state + fresh
    return (result, final_state)


ORDER = (0, 2, 1, 3)
STEPS = ((0,), (1, 7), (2, 6), (3, 5), (4,))


def project_kernel(
    x_ref, wxz_ref, wbd_ref, slot_ref, pool_hbm, cpool_ref,
    xz_out, bc_out, dt_out, h0_out, cc_out,
    xg, sbuf, rbuf, sdt, rdt, pool, st_s, st_r, cc_s, cc_r,
    pool_sem, q_send, q_recv, p_send, p_recv, d_send, d_recv, s_send, s_recv, c_send, c_recv,
):
    r = lax.axis_index("req")
    w = lax.axis_index("wide")
    z = w // 4
    j = w % 4

    def wide_at(zz, jj):
        return zz * 4 + jj

    core_w = wide_at(z, j + 1 - 2 * (j % 2))
    side_w = wide_at(z, (j + 2) % 4)
    up_w = wide_at((z + 1) % 8, j)
    down_w = wide_at((z + 7) % 8, j)

    def xor8(a, v):
        out = 0
        for bit in range(3):
            p = 1 << bit
            ab = a // p % 2
            vb = v // p % 2
            out = out + p * ((ab + vb) % 2)
        return out

    pool_copy = pltpu.make_async_copy(pool_hbm, pool, pool_sem)
    pool_copy.start()

    barrier = pltpu.get_barrier_semaphore()
    for ww in (core_w, side_w, up_w, down_w):
        pl.semaphore_signal(barrier, inc=1, device_id={"req": r, "wide": ww}, device_id_type=MESH)
    for v in range(1, 8):
        pl.semaphore_signal(
            barrier, inc=1, device_id={"req": xor8(r, v), "wide": w}, device_id_type=MESH
        )
    pl.semaphore_wait(barrier, 11)

    counter = [0]

    def send(src, dst, ww):
        i = counter[0]
        counter[0] += 1
        copy = pltpu.make_async_remote_copy(
            src_ref=src, dst_ref=dst, send_sem=q_send.at[i], recv_sem=q_recv.at[i],
            device_id={"req": r, "wide": ww}, device_id_type=MESH,
        )
        copy.start()
        return copy

    copies = []

    def go(src, dst, ww):
        copy = send(src, dst, ww)
        copies.append(copy)
        return copy

    side = go(x_ref, xg.at[0, 1], side_w)
    up0 = go(x_ref, xg.at[1, 0], up_w)
    down0 = go(x_ref, xg.at[7, 0], down_w)
    core0 = go(x_ref, xg.at[0, 2], core_w)
    xg[0, 0] = x_ref[...]

    side.wait_recv()
    up1 = go(xg.at[0, 1], xg.at[1, 1], up_w)
    down1 = go(xg.at[0, 1], xg.at[7, 1], down_w)
    core1 = go(xg.at[0, 1], xg.at[0, 3], core_w)

    pool_copy.wait()

    def state_block(v, i):
        q = xor8(r, v) * 2 + i
        slot = slot_ref[q]
        mine = slot // 8 == r
        local = jnp.clip(slot - r * 8, 0, 7)
        return mine, local

    def fill_state(v):
        m0, l0 = state_block(v, 0)
        m1, l1 = state_block(v, 1)
        st_s[v, 0] = jnp.where(m0, pool[l0], 0.0).astype(BF)
        st_s[v, 1] = jnp.where(m1, pool[l1], 0.0).astype(BF)
        cc_s[v] = jnp.where(m0, cpool_ref[l0, 0], 0.0) + jnp.where(m1, cpool_ref[l1, 1], 0.0)

    def plane_copy(src, dst, ssem, rsem, v):
        return pltpu.make_async_remote_copy(
            src_ref=src, dst_ref=dst, send_sem=ssem, recv_sem=rsem,
            device_id={"req": xor8(r, v), "wide": w}, device_id_type=MESH,
        )

    for v in (1, 2, 3, 4, 5, 6, 7, 0):
        fill_state(v)
        if v:
            plane_copy(st_s.at[v], st_r.at[v], s_send.at[v], s_recv.at[v], v).start()
            plane_copy(cc_s.at[v], cc_r.at[v], c_send.at[v], c_recv.at[v], v).start()

    rows = [pl.multiple_of(xor8(j, q) * 256, 256) for q in ORDER]

    def compute(k):
        zp = (z + 8 - k) % 8
        blocks = [xg[k, p] for p in range(4)]
        for part in range(3):
            def weights(p):
                if part < 2:
                    return wxz_ref[part, pl.ds(rows[p], 256), :]
                return wbd_ref[pl.ds(rows[p], 256), :]

            acc = jnp.dot(blocks[0], weights(0), preferred_element_type=F32)
            for p in range(1, 4):
                acc = acc + jnp.dot(blocks[p], weights(p), preferred_element_type=F32)
            if part < 2:
                sbuf[zp, :, part * 512 : part * 512 + 512] = acc.astype(BF)
            else:
                sbuf[zp, :, 1024:1152] = acc[:, :128].astype(BF)
                sdt[zp] = acc[:, 128:].T[:8]

        @pl.when(zp != 0)
        def _():
            dest = xor8(r, zp)
            for src, dst, ssem, rsem in (
                (sbuf, rbuf, p_send, p_recv), (sdt, rdt, d_send, d_recv),
            ):
                pltpu.make_async_remote_copy(
                    src_ref=src.at[zp], dst_ref=dst.at[zp], send_sem=ssem.at[zp], recv_sem=rsem.at[zp],
                    device_id={"req": dest, "wide": w}, device_id_type=MESH,
                ).start()

    core0.wait_recv()
    core1.wait_recv()
    arrived = {1: (up0, up1), 7: (down0, down1)}
    for step in range(len(STEPS)):
        nxt = STEPS[step + 1] if step + 1 < len(STEPS) else ()
        partner = {}
        later = {}
        for k in nxt:
            for copy in arrived[k]:
                copy.wait_recv()
            partner[k] = go(xg.at[k, 0:2], xg.at[k, 2:4], core_w)
            if k in (1, 2):
                later[k + 1] = (go(xg.at[k, 0:2], xg.at[k + 1, 0:2], up_w),)
            elif k in (7, 6):
                later[k - 1] = (go(xg.at[k, 0:2], xg.at[k - 1, 0:2], down_w),)
            elif k == 3:
                later.setdefault(4, ())
                later[4] += (go(xg.at[3, 0], xg.at[4, 0], up_w),)
            elif k == 5:
                later.setdefault(4, ())
                later[4] += (go(xg.at[5, 1], xg.at[4, 1], down_w),)
        arrived = later
        for k in STEPS[step]:
            compute(k)
        for k in nxt:
            partner[k].wait_recv()

    for copy in copies:
        copy.wait_send()
    for v in range(1, 8):
        for src, dst, ssem, rsem in (
            (sbuf, rbuf, p_send, p_recv), (sdt, rdt, d_send, d_recv),
            (st_s, st_r, s_send, s_recv), (cc_s, cc_r, c_send, c_recv),
        ):
            plane_copy(src.at[v], dst.at[v], ssem.at[v], rsem.at[v], v).wait()

    total = sbuf[0].astype(F32)
    dts = sdt[0]
    caches = cc_s[0]
    for v in range(1, 8):
        total = total + rbuf[v].astype(F32)
        dts = dts + rdt[v]
        caches = caches + cc_r[v]
    xz_out[...] = total[:, :1024].astype(BF)
    bc_out[...] = total[:, 1024:].astype(BF)
    dt_out[...] = dts
    cc_out[...] = caches
    for i in range(2):
        state = st_s[0, i].astype(F32)
        for v in range(1, 8):
            state = state + st_r[v, i].astype(F32)
        h0_out[i] = state


def project(x_t, wxz, wbd, slots, pool, cpool):
    vm = pl.BlockSpec(memory_space=pltpu.VMEM)
    dma = pltpu.SemaphoreType.DMA
    n_q = 7 + 7 + 6
    return pl.pallas_call(
        project_kernel,
        out_shape=(
            jax.ShapeDtypeStruct((256, 1024), BF),
            jax.ShapeDtypeStruct((256, 128), BF),
            jax.ShapeDtypeStruct((8, 256), F32),
            jax.ShapeDtypeStruct((2, 512, 256), F32),
            jax.ShapeDtypeStruct((8, 640), F32),
        ),
        in_specs=[
            vm, vm, vm,
            pl.BlockSpec(memory_space=pltpu.SMEM),
            pl.BlockSpec(memory_space=pl.ANY),
            vm,
        ],
        out_specs=(vm,) * 5,
        scratch_shapes=[
            pltpu.VMEM((8, 4, 256, 256), BF),
            pltpu.VMEM((8, 256, 1152), BF),
            pltpu.VMEM((8, 256, 1152), BF),
            pltpu.VMEM((8, 8, 256), F32),
            pltpu.VMEM((8, 8, 256), F32),
            pltpu.VMEM((8, 512, 256), F32),
            pltpu.VMEM((8, 2, 512, 256), BF),
            pltpu.VMEM((8, 2, 512, 256), BF),
            pltpu.VMEM((8, 8, 640), F32),
            pltpu.VMEM((8, 8, 640), F32),
            dma(()),
            dma((n_q,)), dma((n_q,)),
            dma((8,)), dma((8,)), dma((8,)), dma((8,)),
            dma((8,)), dma((8,)), dma((8,)), dma((8,)),
        ],
        compiler_params=pltpu.CompilerParams(
            collective_id=0, has_side_effects=True, vmem_limit_bytes=50 << 20
        ),
        name="project",
    )(x_t, wxz, wbd, slots, pool, cpool)


def on_device(
    x_in, w_xz, w_dt, w_bc, dt_bias, a_log, d_skip, conv_x_w, conv_x_b, conv_bc_w, conv_bc_b,
    norm_gain, stretch_start, prefix_len, state_slot, ssm_pool, conv_x_pool, conv_bc_pool,
):
    route = []
    for r in range(8):
        for w in range(32):
            f, j = w // 4, w % 4
            route.append((w * 8 + r, ((r ^ f) * 4 + j) * 8 + f))
    x_t = lax.ppermute(x_in, ("wide", "req"), route)
    wxz = jnp.transpose(w_xz, (1, 0, 2))
    wbd = jnp.concatenate([w_bc, w_dt, jnp.zeros((1024, 120), BF)], 1)
    cp = jnp.concatenate([conv_x_pool, conv_bc_pool], 2).astype(F32)
    cpool = jnp.stack(
        [jnp.pad(cp, ((0, 0), (0, 5), (0, 0))), jnp.pad(cp, ((0, 0), (3, 2), (0, 0)))], 1
    )
    xz, bc_raw, dt_t, h0, caches = project(
        x_t, wxz, wbd, state_slot, ssm_pool.reshape(8, 512, 256), cpool
    )
    proj_xz = xz.reshape(256, 2, 512)
    dt_raw = dt_t.T.astype(BF)
    has_cache = (prefix_len > 0).astype(F32)
    start_state = h0.reshape(2, 8, 64, 256) * has_cache[:, None, None, None]
    both = caches[:6].reshape(2, 3, 640) * has_cache[:, None, None]
    cache_x = both[:, :, :512]
    cache_bc = both[:, :, 512:]
    count_tok = 256
    local_heads = 8
    local_width = 512
    member, offset, mask = segments(stretch_start[0], count_tok)
    x_conv = causal_conv(proj_xz[:, 1], cache_x, conv_x_w, conv_x_b, member, offset)
    bc_conv = causal_conv(bc_raw, cache_bc, conv_bc_w, conv_bc_b, member, offset)
    wide_index = lax.axis_index("wide")
    group_span = lax.axis_size("wide") // GROUPS
    bit_total = group_span.bit_length() - 1
    joined = bc_conv
    for bit_index in range(bit_total):
        partner = partner_2(joined, "wide", bit_index)
        upper_half = wide_index // (1 << bit_index) % 2 == 1
        joined = jnp.where(
            upper_half, jnp.concatenate([partner, joined], 1), jnp.concatenate([joined, partner], 1)
        )
    state_width = joined.shape[1] // 2
    b_maps = joined[:, :state_width]
    c_maps = joined[:, state_width:]
    head_width = local_width // local_heads
    result, final_state = mixer(
        x_conv.reshape(count_tok, local_heads, head_width),
        dt_raw, b_maps, c_maps, start_state, member, mask, dt_bias, a_log, d_skip,
    )
    gated = result.reshape(count_tok, local_width) * jax.nn.silu(proj_xz[:, 0].astype(jnp.float32))
    square_sum = jnp.sum(gated * gated, 1)
    for bit_index in range(bit_total):
        square_sum = square_sum + partner_2(square_sum, "wide", bit_index)
    mean_sq = square_sum / (HEADS * HEAD_DIM // GROUPS)
    normed = gated * lax.rsqrt(mean_sq + NORM_EPS)[:, None] * norm_gain[None, :]
    return (normed.astype(jnp.bfloat16), final_state)


def solution(mesh):
    in_specs = (
        P("req", "wide"), P("req", None, "wide"), P("req", "wide"), P("req", "wide"),
        P("wide"), P("wide"), P("wide"), P(None, "wide"), P("wide"), P(None, "wide"),
        P("wide"), P("wide"), P("req", None), P("req"), P(),
        P("req", "wide", None, None), P("req", None, "wide"), P("req", None, "wide"),
    )
    out_specs = (P("req", "wide"), P("req", "wide", None, None))
    return jax.shard_map(
        on_device, mesh=mesh, in_specs=in_specs, out_specs=out_specs, check_vma=False
    )
```

```python
import functools

import jax
import jax.numpy as jnp
from jax import lax
from jax.experimental import pallas as pl
from jax.experimental.pallas import tpu as pltpu
from jax.sharding import PartitionSpec as P

HEADS = 256
HEAD_DIM = 64
GROUPS = 8
NORM_EPS = 1e-05
MESH = pl.DeviceIdType.MESH
BF = jnp.bfloat16
F32 = jnp.float32


ORDER = (0, 2, 1, 3)
STEPS = ((0,), (1, 7), (2, 6), (3, 5), (4,))


XC = 640
YC = 512
XR = 656
YR = 192


def project_kernel(
    x_ref, wxz_ref, wbc_ref, wdt_ref, slot_ref, start_ref, prefix_ref, bias_ref, rate_ref, skip_ref,
    cxw_ref, cxb_ref, cbw_ref, cbb_ref, gain_ref, cxp_ref, cbp_ref, pool_hbm,
    y_out, state_out,
    wbd_ref, cbuf, xsb, xst_ref, ybuf, bcg, ssq,
    b_send, b_recv, n_send, n_recv,
    xg, px, px1, px2, pxs, py, py1, py2, pys, sdt, rdt, pool,
    sx, sx1, sx2, sxs, sy, sy1, sy2, sys,
    pool_sem, q_send, q_recv, d_send, d_recv,
    px1_s, px1_r, px2_s, px2_r, py1_s, py1_r, py2_s, py2_r,
    sx1_s, sx1_r, sx2_s, sx2_r, sy1_s, sy1_r, sy2_s, sy2_r,
):
    r = lax.axis_index("req")
    w = lax.axis_index("wide")
    z = w // 4
    j = w % 4

    def wide_at(zz, jj):
        return zz * 4 + jj

    core_w = wide_at(z, j + 1 - 2 * (j % 2))
    side_w = wide_at(z, (j + 2) % 4)
    up_w = wide_at((z + 1) % 8, j)
    down_w = wide_at((z + 7) % 8, j)

    def xor8(a, v):
        out = 0
        for bit in range(3):
            p = 1 << bit
            ab = a // p % 2
            vb = v // p % 2
            out = out + p * ((ab + vb) % 2)
        return out

    pool_copy = pltpu.make_async_copy(pool_hbm, pool, pool_sem)
    pool_copy.start()

    barrier = pltpu.get_barrier_semaphore()
    quad_w = (w, core_w, side_w, wide_at(z, 3 - j))
    for ww in quad_w[1:] + (up_w, down_w):
        pl.semaphore_signal(barrier, inc=1, device_id={"req": r, "wide": ww}, device_id_type=MESH)
    for v in range(1, 8):
        pl.semaphore_signal(
            barrier, inc=1, device_id={"req": xor8(r, v), "wide": w}, device_id_type=MESH
        )
    pl.semaphore_wait(barrier, 12)

    copies = []

    def go(src, dst, ww):
        i = len(copies)
        copy = pltpu.make_async_remote_copy(
            src_ref=src, dst_ref=dst, send_sem=q_send.at[i], recv_sem=q_recv.at[i],
            device_id={"req": r, "wide": ww}, device_id_type=MESH,
        )
        copy.start()
        copies.append(copy)
        return copy

    def plane(src, dst, ssem, rsem, dest):
        return pltpu.make_async_remote_copy(
            src_ref=src, dst_ref=dst, send_sem=ssem, recv_sem=rsem,
            device_id={"req": dest, "wide": w}, device_id_type=MESH,
        )

    side = go(x_ref, xg.at[0, 1], side_w)
    up0 = go(x_ref, xg.at[1, 0], up_w)
    down0 = go(x_ref, xg.at[7, 0], down_w)
    core0 = go(x_ref, xg.at[0, 2], core_w)
    xg[0, 0] = x_ref[...]

    row8x = lax.broadcasted_iota(jnp.int32, (8, 512), 0)
    row8b = lax.broadcasted_iota(jnp.int32, (8, 128), 0)
    cbuf[15:16, :] = jnp.zeros((1, 256), F32)

    def fill_state(v):
        for i in range(2):
            slot = slot_ref[xor8(r, v) * 2 + i]
            mine = slot // 8 == r
            local = jnp.clip(slot - r * 8, 0, 7)
            sx[v, i * 320 : i * 320 + 320] = jnp.where(mine, pool[local, 0:320], 0.0).astype(BF)
            sy[v, i * YR : i * YR + YR] = jnp.where(mine, pool[local, 320:512], 0.0).astype(BF)
            for m in range(3):
                xrow = jnp.sum(jnp.where(row8x == slot - r * 8, cxp_ref[m].astype(F32), 0.0), 0, keepdims=True)
                brow = jnp.sum(jnp.where(row8b == slot - r * 8, cbp_ref[m].astype(F32), 0.0), 0, keepdims=True)
                e = i * 3 + m
                cbuf[2 * e : 2 * e + 1, :] = xrow[:, :256]
                cbuf[2 * e + 1 : 2 * e + 2, :] = xrow[:, 256:]
                cbuf[12 + e // 2 : 13 + e // 2, e % 2 * 128 : e % 2 * 128 + 128] = brow
        sx[v, 640:656] = cbuf[...].astype(BF)

    def sx_first(vy):
        return plane(sx.at[2 * vy + 1], sx1.at[vy], sx1_s.at[vy], sx1_r.at[vy], xor8(r, 1))

    def sy_first(vy):
        return plane(
            sy.at[pl.ds(2 * vy, 2)], sy1.at[vy], sy1_s.at[vy], sy1_r.at[vy], xor8(r, 2 * vy)
        )

    def sx_second(vy):
        return plane(sxs.at[vy], sx2.at[vy], sx2_s.at[vy], sx2_r.at[vy], xor8(r, 2 * vy))

    def sy_second():
        return plane(sys, sy2, sy2_s, sy2_r, xor8(r, 1))

    wbd_ref[:, :128] = wbc_ref[...]
    wide_dt = jnp.concatenate([wdt_ref[...].astype(F32), jnp.zeros((120, 1024), F32)], 0)
    wbd_ref[:, 128:] = wide_dt.T.astype(BF)

    side.wait_recv()
    up1 = go(xg.at[0, 1], xg.at[1, 1], up_w)
    down1 = go(xg.at[0, 1], xg.at[7, 1], down_w)
    core1 = go(xg.at[0, 1], xg.at[0, 3], core_w)
    pool_copy.wait()
    for vy in (1, 3, 2, 0):
        fill_state(2 * vy + 1)
        sx_first(vy).start()
        fill_state(2 * vy)
        if vy:
            sy_first(vy).start()

    rows = [pl.multiple_of(xor8(j, q) * 256, 256) for q in ORDER]

    def compute(k):
        v = (z + 8 - k) % 8
        vy = v // 2
        vh = v % 2
        blocks = [xg[k, p] for p in range(4)]
        for part in range(3):
            def weights(p):
                if part < 2:
                    return wxz_ref[part, pl.ds(rows[p], 256), :]
                return wbd_ref[pl.ds(rows[p], 256), :]

            acc = jnp.dot(blocks[0], weights(0), preferred_element_type=F32)
            for p in range(1, 4):
                acc = acc + jnp.dot(blocks[p], weights(p), preferred_element_type=F32)
            if part == 0:
                py[v] = acc.astype(BF)
            elif part == 1:
                px[v, :, :512] = acc.astype(BF)
            else:
                px[v, :, 512:] = acc[:, :128].astype(BF)
                sdt[v] = acc[:, 128:].T[:8]

        @pl.when(v != 0)
        def _():
            plane(sdt.at[v], rdt.at[v], d_send.at[v], d_recv.at[v], xor8(r, v)).start()

        @pl.when(vh == 1)
        def _():
            plane(px.at[v], px1.at[vy], px1_s.at[vy], px1_r.at[vy], xor8(r, 1)).start()

        @pl.when(vy != 0)
        def _():
            plane(
                py.at[v], py1.at[v], py1_s.at[v], py1_r.at[v], xor8(r, vy * 2)
            ).start()

    def state_second():
        for vy in (1, 3, 2):
            sx_first(vy).wait()
            sxs[vy] = sx[2 * vy] + sx1[vy]
            sx_second(vy).start()
        for vy in (1, 3, 2):
            sy_first(vy).wait()
        sys[...] = (sy[1] + sy1[1, 1]) + (sy1[2, 1] + sy1[3, 1])
        sy_second().start()

    core0.wait_recv()
    core1.wait_recv()
    arrived = {1: (up0, up1), 7: (down0, down1)}
    for step in range(len(STEPS)):
        nxt = STEPS[step + 1] if step + 1 < len(STEPS) else ()
        partner = {}
        later = {}
        for k in nxt:
            for copy in arrived[k]:
                copy.wait_recv()
            partner[k] = go(xg.at[k, 0:2], xg.at[k, 2:4], core_w)
            if k in (1, 2):
                later[k + 1] = (go(xg.at[k, 0:2], xg.at[k + 1, 0:2], up_w),)
            elif k in (7, 6):
                later[k - 1] = (go(xg.at[k, 0:2], xg.at[k - 1, 0:2], down_w),)
            elif k == 3:
                later[4] = later.get(4, ()) + (go(xg.at[3, 0], xg.at[4, 0], up_w),)
            elif k == 5:
                later[4] = later.get(4, ()) + (go(xg.at[5, 1], xg.at[4, 1], down_w),)
        arrived = later
        for k in STEPS[step]:
            compute(k)
        for k in nxt:
            partner[k].wait_recv()

    state_second()

    def px_first(vy):
        return plane(px.at[2 * vy + 1], px1.at[vy], px1_s.at[vy], px1_r.at[vy], xor8(r, 1))

    def py_first(v):
        return plane(py.at[v], py1.at[v], py1_s.at[v], py1_r.at[v], xor8(r, v // 2 * 2))

    def px_second(vy):
        return plane(pxs.at[vy], px2.at[vy], px2_s.at[vy], px2_r.at[vy], xor8(r, 2 * vy))

    def py_second():
        return plane(pys, py2, py2_s, py2_r, xor8(r, 1))

    for vy in (1, 3, 2):
        px_first(vy).wait()
        pxs[vy] = (px[2 * vy].astype(F32) + px1[vy].astype(F32)).astype(BF)
        px_second(vy).start()
    for v in (3, 5, 7):
        py_first(v).wait()
    pys[...] = (
        (py[1].astype(F32) + py1[3].astype(F32)) + (py1[5].astype(F32) + py1[7].astype(F32))
    ).astype(BF)
    py_second().start()

    for copy in copies:
        copy.wait_send()
    for v in (2, 4, 6):
        py_first(v).wait()
    for v in range(1, 8):
        plane(sdt.at[v], rdt.at[v], d_send.at[v], d_recv.at[v], xor8(r, v)).wait()
    dts = sdt[0]
    for v in range(1, 8):
        dts = dts + rdt[v]
    px_first(0).wait()
    sx_first(0).wait()
    for vy in (1, 3, 2):
        sx_second(vy).wait()
        px_second(vy).wait()
    cbuf[...] = (
        (sx[0, 640:656] + sx1[0, 640:656]) + (sx2[1, 640:656] + sx2[2, 640:656]) + sx2[3, 640:656]
    ).astype(F32)

    start = start_ref[0, 1]
    live = [jnp.where(prefix_ref[i] > 0, 1.0, 0.0) for i in range(2)]

    def total_x(c0, n):
        cols = slice(c0, c0 + n)
        out = px[0, :, cols].astype(F32) + px1[0, :, cols].astype(F32)
        for vy in (1, 2, 3):
            out = out + px2[vy, :, cols].astype(F32)
        return out.astype(BF).astype(F32)

    def conv(values, taps, bias, cache):
        n = values.shape[1]
        tok = lax.broadcasted_iota(jnp.int32, (256, n), 0)
        out = bias + taps[3:4] * values
        for lag in range(1, 4):
            earlier = pltpu.roll(values, lag, 0)
            for i in range(2):
                for o in range(lag):
                    at = o if i == 0 else start + o
                    earlier = jnp.where(tok == at, cache(i, 3 + o - lag), earlier)
            out = out + taps[3 - lag : 4 - lag] * earlier
        return jax.nn.silu(out).astype(BF)

    def cache_b(i, m):
        e = i * 3 + m
        return cbuf[12 + e // 2 : 13 + e // 2, e % 2 * 128 : e % 2 * 128 + 128] * live[i]

    bcg[0] = conv(total_x(512, 128), cbw_ref[...], cbb_ref[...], cache_b)
    shares = []
    for q in range(1, 4):
        copy = pltpu.make_async_remote_copy(
            src_ref=bcg.at[0], dst_ref=bcg.at[q], send_sem=b_send.at[q], recv_sem=b_recv.at[q],
            device_id={"req": r, "wide": quad_w[q]}, device_id_type=MESH,
        )
        copy.start()
        shares.append(copy)

    for half in range(2):
        def cache_x(i, m):
            e = 2 * (i * 3 + m) + half
            return cbuf[e : e + 1, :] * live[i]

        cols = slice(half * 256, half * 256 + 256)
        xs = conv(total_x(half * 256, 256), cxw_ref[:, cols], cxb_ref[:, cols], cache_x)
        xsb[:, cols] = xs
        xst_ref[cols, :] = xs.astype(F32).T

    head = lax.broadcasted_iota(jnp.int32, (8, 256), 0)
    lane = lax.broadcasted_iota(jnp.int32, (8, 256), 1)
    bias8 = jnp.zeros((8, 256), F32)
    rate8 = jnp.zeros((8, 256), F32)
    for h in range(8):
        bias8 = jnp.where(head == h, bias_ref[h], bias8)
        rate8 = jnp.where(head == h, rate_ref[h], rate8)
    raised = dts.astype(BF).astype(F32) + bias8
    step = jnp.maximum(raised, 0.0) + jnp.log1p(jnp.exp(-jnp.abs(raised)))
    rate = -jnp.exp(rate8) * step
    upper_s = lax.broadcasted_iota(jnp.int32, (256, 256), 0)
    upper_t = lax.broadcasted_iota(jnp.int32, (256, 256), 1)
    reach = jnp.where((upper_s <= upper_t) & ((upper_t < start) | (upper_s >= start)), 1.0, 0.0)
    top = rate.astype(BF).astype(F32)
    mid = (rate - top).astype(BF).astype(F32)
    low = rate - top - mid
    parts = jnp.concatenate([top, mid, low, jnp.zeros((8, 256), F32)], 0).astype(BF)
    sums = jnp.dot(parts, reach.astype(BF), preferred_element_type=F32)
    run = sums[0:8] + sums[8:16] + sums[16:24]
    late = lane >= start
    end = [
        jnp.sum(jnp.where(late, 0.0, rate), 1, keepdims=True),
        jnp.sum(jnp.where(late, rate, 0.0), 1, keepdims=True),
    ]
    to_end = jnp.exp(jnp.where(late, end[1], end[0]) - run) * step
    end_decay = [jnp.exp(end[0]), jnp.exp(end[1])]
    columns = jnp.concatenate([run, jnp.exp(run), jnp.zeros((112, 256), F32)], 0).T

    for copy in shares:
        copy.wait()

    def maps(a):
        ab = (a % 2 + j % 2) % 2 + 2 * ((a // 2 + j // 2) % 2)
        return bcg[ab]

    b_maps = jnp.concatenate([maps(0), maps(1)], 1)
    c_maps = jnp.concatenate([maps(2), maps(3)], 1)
    scores = lax.dot_general(
        c_maps, b_maps, (((1,), (1,)), ((), ())), preferred_element_type=F32
    )
    allowed = (upper_t <= upper_s) & ((upper_s < start) | (upper_t >= start))
    scores = jnp.where(allowed, scores, 0.0)
    first = lax.broadcasted_iota(jnp.int32, (256, 128), 1) < 64
    for pair in range(4):
        cols = slice(pair * 128, pair * 128 + 128)
        xs = xsb[:, cols]
        acc = None
        for side_h in range(2):
            h = 2 * pair + side_h
            gap = jnp.minimum(columns[:, h : h + 1] - run[h : h + 1, :], 0.0)
            weight = (jnp.exp(gap) * step[h : h + 1, :] * scores).astype(BF)
            kept = jnp.where(first == (side_h == 0), xs.astype(F32), 0.0).astype(BF)
            part = jnp.dot(weight, kept, preferred_element_type=F32)
            acc = part if acc is None else acc + part
        skip = jnp.where(first, skip_ref[2 * pair], skip_ref[2 * pair + 1])
        ybuf[:, cols] = acc + skip * xs.astype(F32)

    sy_second().wait()
    py_second().wait()

    def h0_piece(i, h):
        if h < 5:
            rows_h = slice(i * 320 + h * 64, i * 320 + h * 64 + 64)
            return (sx[0, rows_h] + sx1[0, rows_h]) + (sx2[1, rows_h] + sx2[2, rows_h]) + sx2[3, rows_h]
        rows_h = slice(i * YR + (h - 5) * 64, i * YR + (h - 5) * 64 + 64)
        return (
            (sy[0, rows_h] + sy1[1, 0, rows_h]) + (sy1[2, 0, rows_h] + sy1[3, 0, rows_h]) + sy2[rows_h]
        )

    square = jnp.zeros((256, 128), F32)
    tok = lax.broadcasted_iota(jnp.int32, (256, 128), 0)
    h0 = [[None] * 8, [None] * 8]
    for pair in range(4):
        cols = slice(pair * 128, pair * 128 + 128)
        from_state = None
        for i in range(2):
            for h in (2 * pair, 2 * pair + 1):
                h0[i][h] = h0_piece(i, h)
            both = jnp.concatenate([h0[i][2 * pair], h0[i][2 * pair + 1]], 0)
            part = lax.dot_general(
                c_maps, both, (((1,), (1,)), ((), ())), preferred_element_type=F32
            ) * live[i]
            from_state = part if i == 0 else jnp.where(tok >= start, part, from_state)
        grown = jnp.where(
            first, columns[:, 8 + 2 * pair : 9 + 2 * pair], columns[:, 9 + 2 * pair : 10 + 2 * pair]
        )
        result = ybuf[:, cols] + from_state * grown
        gate = py[0, :, cols].astype(F32) + py2[:, cols].astype(F32)
        for v in (2, 4, 6):
            gate = gate + py1[v, :, cols].astype(F32)
        gated = result * jax.nn.silu(gate.astype(BF).astype(F32))
        ybuf[:, cols] = gated
        square = square + gated * gated

    ssq[0] = jnp.broadcast_to(jnp.sum(square.T, 0, keepdims=True), (8, 256))
    norms = []
    for q in range(1, 4):
        copy = pltpu.make_async_remote_copy(
            src_ref=ssq.at[0], dst_ref=ssq.at[q], send_sem=n_send.at[q], recv_sem=n_recv.at[q],
            device_id={"req": r, "wide": quad_w[q]}, device_id_type=MESH,
        )
        copy.start()
        norms.append(copy)

    for h in range(8):
        rows_h = slice(h * 64, h * 64 + 64)
        spread = xst_ref[rows_h, :] * to_end[h : h + 1, :]
        late_row = lax.broadcasted_iota(jnp.int32, (64, 256), 1) >= start
        for i in range(2):
            u = jnp.where(late_row == (i == 1), spread, 0.0).astype(BF)
            fresh = jnp.dot(u, b_maps, preferred_element_type=F32)
            keep = end_decay[i][h : h + 1, :] * live[i]
            state_out[i, rows_h, :] = keep * h0[i][h].astype(F32) + fresh

    for copy in norms:
        copy.wait()
    mean = (ssq[0] + ssq[1] + ssq[2] + ssq[3]) / (HEADS * HEAD_DIM // GROUPS)
    scale = jnp.broadcast_to(lax.rsqrt(mean + NORM_EPS)[0:1], (128, 256)).T
    for pair in range(4):
        cols = slice(pair * 128, pair * 128 + 128)
        y_out[:, cols] = (ybuf[:, cols] * scale * gain_ref[:, cols]).astype(BF)


def project(*args):
    vm = pl.BlockSpec(memory_space=pltpu.VMEM)
    sm = pl.BlockSpec(memory_space=pltpu.SMEM)
    dma = pltpu.SemaphoreType.DMA
    n_q = 7 + 7 + 6
    return pl.pallas_call(
        project_kernel,
        out_shape=(
            jax.ShapeDtypeStruct((256, 512), BF),
            jax.ShapeDtypeStruct((2, 512, 256), F32),
        ),
        in_specs=[vm] * 4 + [sm] * 6 + [vm] * 7 + [pl.BlockSpec(memory_space=pl.ANY)],
        out_specs=(vm,) * 2,
        scratch_shapes=[
            pltpu.VMEM((1024, 256), BF),
            pltpu.VMEM((16, 256), F32),
            pltpu.VMEM((256, 512), BF),
            pltpu.VMEM((512, 256), F32),
            pltpu.VMEM((256, 512), F32),
            pltpu.VMEM((4, 256, 128), BF),
            pltpu.VMEM((4, 8, 256), F32),
            dma((4,)), dma((4,)), dma((4,)), dma((4,)),
            pltpu.VMEM((8, 4, 256, 256), BF),
            pltpu.VMEM((8, 256, XC), BF),
            pltpu.VMEM((4, 256, XC), BF),
            pltpu.VMEM((4, 256, XC), BF),
            pltpu.VMEM((4, 256, XC), BF),
            pltpu.VMEM((8, 256, YC), BF),
            pltpu.VMEM((8, 256, YC), BF),
            pltpu.VMEM((256, YC), BF),
            pltpu.VMEM((256, YC), BF),
            pltpu.VMEM((8, 8, 256), F32),
            pltpu.VMEM((8, 8, 256), F32),
            pltpu.VMEM((8, 512, 256), F32),
            pltpu.VMEM((8, XR, 256), BF),
            pltpu.VMEM((4, XR, 256), BF),
            pltpu.VMEM((4, XR, 256), BF),
            pltpu.VMEM((4, XR, 256), BF),
            pltpu.VMEM((8, 2 * YR, 256), BF),
            pltpu.VMEM((4, 2, 2 * YR, 256), BF),
            pltpu.VMEM((2 * YR, 256), BF),
            pltpu.VMEM((2 * YR, 256), BF),
            dma(()),
            dma((n_q,)), dma((n_q,)), dma((8,)), dma((8,)),
            dma((4,)), dma((4,)), dma((4,)), dma((4,)), dma((8,)), dma((8,)), dma(()), dma(()),
            dma((4,)), dma((4,)), dma((4,)), dma((4,)), dma((4,)), dma((4,)), dma(()), dma(()),
        ],
        compiler_params=pltpu.CompilerParams(
            collective_id=0, has_side_effects=True, vmem_limit_bytes=56 << 20
        ),
        name="project",
    )(*args)


def on_device(
    x_in, w_xz, w_dt, w_bc, dt_bias, a_log, d_skip, conv_x_w, conv_x_b, conv_bc_w, conv_bc_b,
    norm_gain, stretch_start, prefix_len, state_slot, ssm_pool, conv_x_pool, conv_bc_pool,
):
    route = []
    for r in range(8):
        for w in range(32):
            f, j = w // 4, w % 4
            route.append((w * 8 + r, ((r ^ f) * 4 + j) * 8 + f))
    x_t = lax.ppermute(x_in, ("wide", "req"), route)
    y, state = project(
        x_t, jnp.transpose(w_xz, (1, 0, 2)), w_bc, w_dt.T,
        state_slot, stretch_start, prefix_len, dt_bias, a_log, d_skip,
        conv_x_w, conv_x_b[None], conv_bc_w, conv_bc_b[None], norm_gain[None],
        jnp.transpose(conv_x_pool, (1, 0, 2)), jnp.transpose(conv_bc_pool, (1, 0, 2)),
        ssm_pool.reshape(8, 512, 256),
    )
    return y, state.reshape(2, 8, 64, 256)


def solution(mesh):
    in_specs = (
        P("req", "wide"), P("req", None, "wide"), P("req", "wide"), P("req", "wide"),
        P("wide"), P("wide"), P("wide"), P(None, "wide"), P("wide"), P(None, "wide"),
        P("wide"), P("wide"), P("req", None), P("req"), P(),
        P("req", "wide", None, None), P("req", None, "wide"), P("req", None, "wide"),
    )
    out_specs = (P("req", "wide"), P("req", "wide", None, None))
    return jax.shard_map(
        on_device, mesh=mesh, in_specs=in_specs, out_specs=out_specs, check_vma=False
    )
```

```python
import functools

import jax
import jax.numpy as jnp
from jax import lax
from jax.experimental import pallas as pl
from jax.experimental.pallas import tpu as pltpu
from jax.sharding import PartitionSpec as P

HEADS = 256
HEAD_DIM = 64
GROUPS = 8
NORM_EPS = 1e-05
MESH = pl.DeviceIdType.MESH
BF = jnp.bfloat16
F32 = jnp.float32


ORDER = (0, 2, 1, 3)
STEPS = ((0,), (1, 7), (2, 6), (3, 5), (4,))


XC = 640
YC = 512
XR = 400
YR = 320
CUT = 208


def project_kernel(
    x_ref, wxz_ref, wbc_ref, wdt_ref, slot_ref, start_ref, prefix_ref, bias_ref, rate_ref, skip_ref,
    cxw_ref, cxb_ref, cbw_ref, cbb_ref, gain_ref, cxp_ref, cbp_ref, pool_hbm,
    y_out, state_out,
    wbd_ref, cbuf, xsb, xst_ref, ybuf, bcg, ssq,
    b_send, b_recv, n_send, n_recv, via_sy, via_sx, via_px, via_s, via_r,
    xg, px, px1, px2, pxs, py, py1, py2, pys, sdt, rdt, pool,
    sx, sx1, sx2, sxs, sy, sy1, sy2, sys,
    pool_sem, q_send, q_recv, d_send, d_recv,
    px1_s, px1_r, px2_s, px2_r, py1_s, py1_r, py2_s, py2_r,
    sx1_s, sx1_r, sx2_s, sx2_r, sy1_s, sy1_r, sy2_s, sy2_r,
):
    r = lax.axis_index("req")
    w = lax.axis_index("wide")
    z = w // 4
    j = w % 4

    def wide_at(zz, jj):
        return zz * 4 + jj

    core_w = wide_at(z, j + 1 - 2 * (j % 2))
    side_w = wide_at(z, (j + 2) % 4)
    up_w = wide_at((z + 1) % 8, j)
    down_w = wide_at((z + 7) % 8, j)

    def xor8(a, v):
        out = 0
        for bit in range(3):
            p = 1 << bit
            ab = a // p % 2
            vb = v // p % 2
            out = out + p * ((ab + vb) % 2)
        return out

    pool_copy = pltpu.make_async_copy(pool_hbm, pool, pool_sem)
    pool_copy.start()

    barrier = pltpu.get_barrier_semaphore()
    quad_w = (w, core_w, side_w, wide_at(z, 3 - j))
    for ww in quad_w[1:] + (up_w, down_w):
        pl.semaphore_signal(barrier, inc=1, device_id={"req": r, "wide": ww}, device_id_type=MESH)
    for v in range(1, 8):
        pl.semaphore_signal(
            barrier, inc=1, device_id={"req": xor8(r, v), "wide": w}, device_id_type=MESH
        )
    pl.semaphore_wait(barrier, 12)

    copies = []

    def go(src, dst, ww):
        i = len(copies)
        copy = pltpu.make_async_remote_copy(
            src_ref=src, dst_ref=dst, send_sem=q_send.at[i], recv_sem=q_recv.at[i],
            device_id={"req": r, "wide": ww}, device_id_type=MESH,
        )
        copy.start()
        copies.append(copy)
        return copy

    def plane(src, dst, ssem, rsem, dest):
        return pltpu.make_async_remote_copy(
            src_ref=src, dst_ref=dst, send_sem=ssem, recv_sem=rsem,
            device_id={"req": dest, "wide": w}, device_id_type=MESH,
        )

    side = go(x_ref, xg.at[0, 1], side_w)
    up0 = go(x_ref, xg.at[1, 0], up_w)
    down0 = go(x_ref, xg.at[7, 0], down_w)
    core0 = go(x_ref, xg.at[0, 2], core_w)
    xg[0, 0] = x_ref[...]

    row8x = lax.broadcasted_iota(jnp.int32, (8, 512), 0)
    row8b = lax.broadcasted_iota(jnp.int32, (8, 128), 0)
    cbuf[15:16, :] = jnp.zeros((1, 256), F32)

    def fill_state(v):
        for i in range(2):
            slot = slot_ref[xor8(r, v) * 2 + i]
            mine = slot // 8 == r
            local = jnp.clip(slot - r * 8, 0, 7)
            sx[v, i * 192 : i * 192 + 192] = jnp.where(mine, pool[local, 0:192], 0.0).astype(BF)
            sy[v, i * YR : i * YR + YR] = jnp.where(mine, pool[local, 192:512], 0.0).astype(BF)
            for m in range(3):
                xrow = jnp.sum(jnp.where(row8x == slot - r * 8, cxp_ref[m].astype(F32), 0.0), 0, keepdims=True)
                brow = jnp.sum(jnp.where(row8b == slot - r * 8, cbp_ref[m].astype(F32), 0.0), 0, keepdims=True)
                e = i * 3 + m
                cbuf[2 * e : 2 * e + 1, :] = xrow[:, :256]
                cbuf[2 * e + 1 : 2 * e + 2, :] = xrow[:, 256:]
                cbuf[12 + e // 2 : 13 + e // 2, e % 2 * 128 : e % 2 * 128 + 128] = brow
        sx[v, 384:400] = cbuf[...].astype(BF)

    def sx_first(vy):
        return plane(sx.at[2 * vy + 1], sx1.at[vy], sx1_s.at[vy], sx1_r.at[vy], xor8(r, 1))

    def sy_first(vy):
        return plane(
            sy.at[pl.ds(2 * vy, 2)], sy1.at[vy], sy1_s.at[vy], sy1_r.at[vy], xor8(r, 2 * vy)
        )

    def sx_second(vy):
        return plane(sxs.at[vy], sx2.at[vy], sx2_s.at[vy], sx2_r.at[vy], xor8(r, 2 * vy))

    def sy_second():
        return plane(sys, sy2, sy2_s, sy2_r, xor8(r, 1))

    wbd_ref[:, :128] = wbc_ref[...]
    wide_dt = jnp.concatenate([wdt_ref[...].astype(F32), jnp.zeros((120, 1024), F32)], 0)
    wbd_ref[:, 128:] = wide_dt.T.astype(BF)

    side.wait_recv()
    up1 = go(xg.at[0, 1], xg.at[1, 1], up_w)
    down1 = go(xg.at[0, 1], xg.at[7, 1], down_w)
    core1 = go(xg.at[0, 1], xg.at[0, 3], core_w)
    pool_copy.wait()
    def via(n, src, dst):
        return plane(src, dst, via_s.at[n], via_r.at[n], xor8(r, 2 + 4 * (n % 2)))

    def sy_via(n):
        return via(n, sy.at[4 + n], via_sy.at[n])

    for vy in (2, 1, 3, 0):
        fill_state(2 * vy)
        fill_state(2 * vy + 1)
        if vy == 2:
            sy_via(0).start()
            sy_via(1).start()
        sx_first(vy).start()

    def state_join():
        for n, own, vy in ((0, 6, 3), (1, 3, 1)):
            sy_via(n).wait()
            sy[own] = sy[own] + via_sy[n]
            sy_first(vy).start()

    rows = [pl.multiple_of(xor8(j, q) * 256, 256) for q in ORDER]

    def compute(k):
        v = (z + 8 - k) % 8
        vy = v // 2
        vh = v % 2
        blocks = [xg[k, p] for p in range(4)]
        for part in range(3):
            def weights(p):
                if part < 2:
                    return wxz_ref[part, pl.ds(rows[p], 256), :]
                return wbd_ref[pl.ds(rows[p], 256), :]

            acc = jnp.dot(blocks[0], weights(0), preferred_element_type=F32)
            for p in range(1, 4):
                acc = acc + jnp.dot(blocks[p], weights(p), preferred_element_type=F32)
            if part == 0:
                py[v] = acc.astype(BF)
            elif part == 1:
                px[v, :, :512] = acc.astype(BF)
            else:
                px[v, :, 512:] = acc[:, :128].astype(BF)
                sdt[v] = acc[:, 128:].T[:8]

        @pl.when(v != 0)
        def _():
            plane(sdt.at[v], rdt.at[v], d_send.at[v], d_recv.at[v], xor8(r, v)).start()

        @pl.when(vh == 1)
        def _():
            plane(px.at[v], px1.at[vy], px1_s.at[vy], px1_r.at[vy], xor8(r, 1)).start()

        @pl.when(vy != 0)
        def _():
            plane(
                py.at[v], py1.at[v], py1_s.at[v], py1_r.at[v], xor8(r, vy * 2)
            ).start()

    def sx_via(n):
        part = slice(0, CUT) if n == 0 else slice(CUT, XR)
        return via(2 + n, sxs.at[2, part], via_sx.at[part])

    def state_second():
        sx_first(2).wait()
        sxs[2] = sx[4] + sx1[2]
        sx_via(0).start()
        sx_via(1).start()
        for vy in (1, 3):
            sx_first(vy).wait()
            sxs[vy] = sx[2 * vy] + sx1[vy]
        for vy in (1, 3):
            sy_first(vy).wait()
        sys[...] = (sy[1] + sy1[1, 1]) + sy1[3, 1]
        sy_second().start()

    def state_third():
        sx_via(0).wait()
        sxs[3, :CUT] = sxs[3, :CUT] + via_sx[:CUT]
        sx_second(3).start()
        sx_via(1).wait()
        sxs[1, CUT:] = sxs[1, CUT:] + via_sx[CUT:]
        sx_second(1).start()

    core0.wait_recv()
    core1.wait_recv()
    arrived = {1: (up0, up1), 7: (down0, down1)}
    for step in range(len(STEPS)):
        nxt = STEPS[step + 1] if step + 1 < len(STEPS) else ()
        partner = {}
        later = {}
        for k in nxt:
            for copy in arrived[k]:
                copy.wait_recv()
            partner[k] = go(xg.at[k, 0:2], xg.at[k, 2:4], core_w)
            if k in (1, 2):
                later[k + 1] = (go(xg.at[k, 0:2], xg.at[k + 1, 0:2], up_w),)
            elif k in (7, 6):
                later[k - 1] = (go(xg.at[k, 0:2], xg.at[k - 1, 0:2], down_w),)
            elif k == 3:
                later[4] = later.get(4, ()) + (go(xg.at[3, 0], xg.at[4, 0], up_w),)
            elif k == 5:
                later[4] = later.get(4, ()) + (go(xg.at[5, 1], xg.at[4, 1], down_w),)
        arrived = later
        for k in STEPS[step]:
            compute(k)
        if step == 0:
            state_join()
        for k in nxt:
            partner[k].wait_recv()

    state_second()

    def px_first(vy):
        return plane(px.at[2 * vy + 1], px1.at[vy], px1_s.at[vy], px1_r.at[vy], xor8(r, 1))

    def py_first(v):
        return plane(py.at[v], py1.at[v], py1_s.at[v], py1_r.at[v], xor8(r, v // 2 * 2))

    def px_second(vy):
        return plane(pxs.at[vy], px2.at[vy], px2_s.at[vy], px2_r.at[vy], xor8(r, 2 * vy))

    def py_second():
        return plane(pys, py2, py2_s, py2_r, xor8(r, 1))

    def px_via(n):
        part = slice(128 * n, 128 * n + 128)
        return via(4 + n, pxs.at[2, part], via_px.at[part])

    px_first(2).wait()
    pxs[2] = (px[4].astype(F32) + px1[2].astype(F32)).astype(BF)
    px_via(0).start()
    px_via(1).start()
    state_third()
    for n, vy in ((0, 3), (1, 1)):
        px_first(vy).wait()
        px_via(n).wait()
        part = slice(128 * n, 128 * n + 128)
        rest = slice(128 - 128 * n, 256 - 128 * n)
        joined = px[2 * vy, part].astype(F32) + px1[vy, part].astype(F32) + via_px[part].astype(F32)
        pxs[vy, part] = joined.astype(BF)
        pxs[vy, rest] = (px[2 * vy, rest].astype(F32) + px1[vy, rest].astype(F32)).astype(BF)
        px_second(vy).start()
    for v in (3, 5, 7):
        py_first(v).wait()
    pys[...] = (
        (py[1].astype(F32) + py1[3].astype(F32)) + (py1[5].astype(F32) + py1[7].astype(F32))
    ).astype(BF)
    py_second().start()

    for copy in copies:
        copy.wait_send()
    for v in (2, 4, 6):
        py_first(v).wait()
    for v in range(1, 8):
        plane(sdt.at[v], rdt.at[v], d_send.at[v], d_recv.at[v], xor8(r, v)).wait()
    dts = sdt[0]
    for v in range(1, 8):
        dts = dts + rdt[v]
    px_first(0).wait()
    sx_first(0).wait()
    for vy in (1, 3):
        sx_second(vy).wait()
        px_second(vy).wait()
    cbuf[...] = (
        (sx[0, 384:400] + sx1[0, 384:400]) + (sx2[1, 384:400] + sx2[3, 384:400])
    ).astype(F32)

    start = start_ref[0, 1]
    live = [jnp.where(prefix_ref[i] > 0, 1.0, 0.0) for i in range(2)]

    def total_x(c0, n):
        cols = slice(c0, c0 + n)
        out = px[0, :, cols].astype(F32) + px1[0, :, cols].astype(F32)
        for vy in (1, 3):
            out = out + px2[vy, :, cols].astype(F32)
        return out.astype(BF).astype(F32)

    def conv(values, taps, bias, cache):
        n = values.shape[1]
        tok = lax.broadcasted_iota(jnp.int32, (256, n), 0)
        out = bias + taps[3:4] * values
        for lag in range(1, 4):
            earlier = pltpu.roll(values, lag, 0)
            for i in range(2):
                for o in range(lag):
                    at = o if i == 0 else start + o
                    earlier = jnp.where(tok == at, cache(i, 3 + o - lag), earlier)
            out = out + taps[3 - lag : 4 - lag] * earlier
        return jax.nn.silu(out).astype(BF)

    def cache_b(i, m):
        e = i * 3 + m
        return cbuf[12 + e // 2 : 13 + e // 2, e % 2 * 128 : e % 2 * 128 + 128] * live[i]

    bcg[0] = conv(total_x(512, 128), cbw_ref[...], cbb_ref[...], cache_b)
    shares = []
    for q in range(1, 4):
        copy = pltpu.make_async_remote_copy(
            src_ref=bcg.at[0], dst_ref=bcg.at[q], send_sem=b_send.at[q], recv_sem=b_recv.at[q],
            device_id={"req": r, "wide": quad_w[q]}, device_id_type=MESH,
        )
        copy.start()
        shares.append(copy)

    for half in range(2):
        def cache_x(i, m):
            e = 2 * (i * 3 + m) + half
            return cbuf[e : e + 1, :] * live[i]

        cols = slice(half * 256, half * 256 + 256)
        xs = conv(total_x(half * 256, 256), cxw_ref[:, cols], cxb_ref[:, cols], cache_x)
        xsb[:, cols] = xs
        xst_ref[cols, :] = xs.astype(F32).T

    head = lax.broadcasted_iota(jnp.int32, (8, 256), 0)
    lane = lax.broadcasted_iota(jnp.int32, (8, 256), 1)
    bias8 = jnp.zeros((8, 256), F32)
    rate8 = jnp.zeros((8, 256), F32)
    for h in range(8):
        bias8 = jnp.where(head == h, bias_ref[h], bias8)
        rate8 = jnp.where(head == h, rate_ref[h], rate8)
    raised = dts.astype(BF).astype(F32) + bias8
    step = jnp.maximum(raised, 0.0) + jnp.log1p(jnp.exp(-jnp.abs(raised)))
    rate = -jnp.exp(rate8) * step
    upper_s = lax.broadcasted_iota(jnp.int32, (256, 256), 0)
    upper_t = lax.broadcasted_iota(jnp.int32, (256, 256), 1)
    reach = jnp.where((upper_s <= upper_t) & ((upper_t < start) | (upper_s >= start)), 1.0, 0.0)
    top = rate.astype(BF).astype(F32)
    mid = (rate - top).astype(BF).astype(F32)
    low = rate - top - mid
    parts = jnp.concatenate([top, mid, low, jnp.zeros((8, 256), F32)], 0).astype(BF)
    sums = jnp.dot(parts, reach.astype(BF), preferred_element_type=F32)
    run = sums[0:8] + sums[8:16] + sums[16:24]
    late = lane >= start
    end = [
        jnp.sum(jnp.where(late, 0.0, rate), 1, keepdims=True),
        jnp.sum(jnp.where(late, rate, 0.0), 1, keepdims=True),
    ]
    to_end = jnp.exp(jnp.where(late, end[1], end[0]) - run) * step
    end_decay = [jnp.exp(end[0]), jnp.exp(end[1])]
    columns = jnp.concatenate([run, jnp.exp(run), jnp.zeros((112, 256), F32)], 0).T

    for copy in shares:
        copy.wait()

    def maps(a):
        ab = (a % 2 + j % 2) % 2 + 2 * ((a // 2 + j // 2) % 2)
        return bcg[ab]

    b_maps = jnp.concatenate([maps(0), maps(1)], 1)
    c_maps = jnp.concatenate([maps(2), maps(3)], 1)
    scores = lax.dot_general(
        c_maps, b_maps, (((1,), (1,)), ((), ())), preferred_element_type=F32
    )
    allowed = (upper_t <= upper_s) & ((upper_s < start) | (upper_t >= start))
    scores = jnp.where(allowed, scores, 0.0)
    first = lax.broadcasted_iota(jnp.int32, (256, 128), 1) < 64
    for pair in range(4):
        cols = slice(pair * 128, pair * 128 + 128)
        xs = xsb[:, cols]
        acc = None
        for side_h in range(2):
            h = 2 * pair + side_h
            gap = jnp.minimum(columns[:, h : h + 1] - run[h : h + 1, :], 0.0)
            weight = (jnp.exp(gap) * step[h : h + 1, :] * scores).astype(BF)
            kept = jnp.where(first == (side_h == 0), xs.astype(F32), 0.0).astype(BF)
            part = jnp.dot(weight, kept, preferred_element_type=F32)
            acc = part if acc is None else acc + part
        skip = jnp.where(first, skip_ref[2 * pair], skip_ref[2 * pair + 1])
        ybuf[:, cols] = acc + skip * xs.astype(F32)

    sy_second().wait()
    py_second().wait()

    def h0_piece(i, h):
        if h < 3:
            rows_h = slice(i * 192 + h * 64, i * 192 + h * 64 + 64)
            return (sx[0, rows_h] + sx1[0, rows_h]) + (sx2[1, rows_h] + sx2[3, rows_h])
        rows_h = slice(i * YR + (h - 3) * 64, i * YR + (h - 3) * 64 + 64)
        return (
            (sy[0, rows_h] + sy1[1, 0, rows_h]) + (sy1[3, 0, rows_h] + sy2[rows_h])
        )

    square = jnp.zeros((256, 128), F32)
    tok = lax.broadcasted_iota(jnp.int32, (256, 128), 0)
    h0 = [[None] * 8, [None] * 8]
    for pair in range(4):
        cols = slice(pair * 128, pair * 128 + 128)
        from_state = None
        for i in range(2):
            for h in (2 * pair, 2 * pair + 1):
                h0[i][h] = h0_piece(i, h)
            both = jnp.concatenate([h0[i][2 * pair], h0[i][2 * pair + 1]], 0)
            part = lax.dot_general(
                c_maps, both, (((1,), (1,)), ((), ())), preferred_element_type=F32
            ) * live[i]
            from_state = part if i == 0 else jnp.where(tok >= start, part, from_state)
        grown = jnp.where(
            first, columns[:, 8 + 2 * pair : 9 + 2 * pair], columns[:, 9 + 2 * pair : 10 + 2 * pair]
        )
        result = ybuf[:, cols] + from_state * grown
        gate = py[0, :, cols].astype(F32) + py2[:, cols].astype(F32)
        for v in (2, 4, 6):
            gate = gate + py1[v, :, cols].astype(F32)
        gated = result * jax.nn.silu(gate.astype(BF).astype(F32))
        ybuf[:, cols] = gated
        square = square + gated * gated

    ssq[0] = jnp.broadcast_to(jnp.sum(square.T, 0, keepdims=True), (8, 256))
    norms = []
    for q in range(1, 4):
        copy = pltpu.make_async_remote_copy(
            src_ref=ssq.at[0], dst_ref=ssq.at[q], send_sem=n_send.at[q], recv_sem=n_recv.at[q],
            device_id={"req": r, "wide": quad_w[q]}, device_id_type=MESH,
        )
        copy.start()
        norms.append(copy)

    for h in range(8):
        rows_h = slice(h * 64, h * 64 + 64)
        spread = xst_ref[rows_h, :] * to_end[h : h + 1, :]
        late_row = lax.broadcasted_iota(jnp.int32, (64, 256), 1) >= start
        for i in range(2):
            u = jnp.where(late_row == (i == 1), spread, 0.0).astype(BF)
            fresh = jnp.dot(u, b_maps, preferred_element_type=F32)
            keep = end_decay[i][h : h + 1, :] * live[i]
            state_out[i, rows_h, :] = keep * h0[i][h].astype(F32) + fresh

    for copy in norms:
        copy.wait()
    mean = (ssq[0] + ssq[1] + ssq[2] + ssq[3]) / (HEADS * HEAD_DIM // GROUPS)
    scale = jnp.broadcast_to(lax.rsqrt(mean + NORM_EPS)[0:1], (128, 256)).T
    for pair in range(4):
        cols = slice(pair * 128, pair * 128 + 128)
        y_out[:, cols] = (ybuf[:, cols] * scale * gain_ref[:, cols]).astype(BF)


def project(*args):
    vm = pl.BlockSpec(memory_space=pltpu.VMEM)
    sm = pl.BlockSpec(memory_space=pltpu.SMEM)
    dma = pltpu.SemaphoreType.DMA
    n_q = 7 + 7 + 6
    return pl.pallas_call(
        project_kernel,
        out_shape=(
            jax.ShapeDtypeStruct((256, 512), BF),
            jax.ShapeDtypeStruct((2, 512, 256), F32),
        ),
        in_specs=[vm] * 4 + [sm] * 6 + [vm] * 7 + [pl.BlockSpec(memory_space=pl.ANY)],
        out_specs=(vm,) * 2,
        scratch_shapes=[
            pltpu.VMEM((1024, 256), BF),
            pltpu.VMEM((16, 256), F32),
            pltpu.VMEM((256, 512), BF),
            pltpu.VMEM((512, 256), F32),
            pltpu.VMEM((256, 512), F32),
            pltpu.VMEM((4, 256, 128), BF),
            pltpu.VMEM((4, 8, 256), F32),
            dma((4,)), dma((4,)), dma((4,)), dma((4,)),
            pltpu.VMEM((2, 2 * YR, 256), BF),
            pltpu.VMEM((XR, 256), BF),
            pltpu.VMEM((256, XC), BF),
            dma((6,)), dma((6,)),
            pltpu.VMEM((8, 4, 256, 256), BF),
            pltpu.VMEM((8, 256, XC), BF),
            pltpu.VMEM((4, 256, XC), BF),
            pltpu.VMEM((4, 256, XC), BF),
            pltpu.VMEM((4, 256, XC), BF),
            pltpu.VMEM((8, 256, YC), BF),
            pltpu.VMEM((8, 256, YC), BF),
            pltpu.VMEM((256, YC), BF),
            pltpu.VMEM((256, YC), BF),
            pltpu.VMEM((8, 8, 256), F32),
            pltpu.VMEM((8, 8, 256), F32),
            pltpu.VMEM((8, 512, 256), F32),
            pltpu.VMEM((8, XR, 256), BF),
            pltpu.VMEM((4, XR, 256), BF),
            pltpu.VMEM((4, XR, 256), BF),
            pltpu.VMEM((4, XR, 256), BF),
            pltpu.VMEM((8, 2 * YR, 256), BF),
            pltpu.VMEM((4, 2, 2 * YR, 256), BF),
            pltpu.VMEM((2 * YR, 256), BF),
            pltpu.VMEM((2 * YR, 256), BF),
            dma(()),
            dma((n_q,)), dma((n_q,)), dma((8,)), dma((8,)),
            dma((4,)), dma((4,)), dma((4,)), dma((4,)), dma((8,)), dma((8,)), dma(()), dma(()),
            dma((4,)), dma((4,)), dma((4,)), dma((4,)), dma((4,)), dma((4,)), dma(()), dma(()),
        ],
        compiler_params=pltpu.CompilerParams(
            collective_id=0, has_side_effects=True, vmem_limit_bytes=56 << 20
        ),
        name="project",
    )(*args)


def on_device(
    x_in, w_xz, w_dt, w_bc, dt_bias, a_log, d_skip, conv_x_w, conv_x_b, conv_bc_w, conv_bc_b,
    norm_gain, stretch_start, prefix_len, state_slot, ssm_pool, conv_x_pool, conv_bc_pool,
):
    route = []
    for r in range(8):
        for w in range(32):
            f, j = w // 4, w % 4
            route.append((w * 8 + r, ((r ^ f) * 4 + j) * 8 + f))
    x_t = lax.ppermute(x_in, ("wide", "req"), route)
    y, state = project(
        x_t, jnp.transpose(w_xz, (1, 0, 2)), w_bc, w_dt.T,
        state_slot, stretch_start, prefix_len, dt_bias, a_log, d_skip,
        conv_x_w, conv_x_b[None], conv_bc_w, conv_bc_b[None], norm_gain[None],
        jnp.transpose(conv_x_pool, (1, 0, 2)), jnp.transpose(conv_bc_pool, (1, 0, 2)),
        ssm_pool.reshape(8, 512, 256),
    )
    return y, state.reshape(2, 8, 64, 256)


def solution(mesh):
    in_specs = (
        P("req", "wide"), P("req", None, "wide"), P("req", "wide"), P("req", "wide"),
        P("wide"), P("wide"), P("wide"), P(None, "wide"), P("wide"), P(None, "wide"),
        P("wide"), P("wide"), P("req", None), P("req"), P(),
        P("req", "wide", None, None), P("req", None, "wide"), P("req", None, "wide"),
    )
    out_specs = (P("req", "wide"), P("req", "wide", None, None))
    return jax.shard_map(
        on_device, mesh=mesh, in_specs=in_specs, out_specs=out_specs, check_vma=False
    )
```

```python
import functools

import jax
import jax.numpy as jnp
from jax import lax
from jax.experimental import pallas as pl
from jax.experimental.pallas import tpu as pltpu
from jax.sharding import PartitionSpec as P

HEADS = 256
HEAD_DIM = 64
GROUPS = 8
NORM_EPS = 1e-05
MESH = pl.DeviceIdType.MESH
BF = jnp.bfloat16
F32 = jnp.float32


ORDER = (0, 2, 1, 3)
STEPS = ((0,), (1, 7), (2, 6), (3, 5), (4,))


XC = 640
YC = 512
XR = 400
YR = 320
CUT = 208


def project_kernel(
    x_ref, wxz_ref, wbc_ref, wdt_ref, slot_ref, start_ref, prefix_ref, bias_ref, rate_ref, skip_ref,
    cxw_ref, cxb_ref, cbw_ref, cbb_ref, gain_ref, cxp_ref, cbp_ref, pool_hbm,
    y_out, state_out,
    wbd_ref, cbuf, xsb, xst_ref, ybuf, bcg, ssq,
    b_send, b_recv, n_send, n_recv, via_sy, via_sx, via_px, via_s, via_r,
    xg, px, px1, px2, pxs, py, py1, py2, pys, sdt, rdt, pool,
    sx, sx1, sx2, sxs, sy, sy1, sy2, sys,
    pool_sem, q_send, q_recv, d_send, d_recv,
    px1_s, px1_r, px2_s, px2_r, py1_s, py1_r, py2_s, py2_r,
    sx1_s, sx1_r, sx2_s, sx2_r, sy1_s, sy1_r, sy2_s, sy2_r,
):
    r = lax.axis_index("req")
    w = lax.axis_index("wide")
    z = w // 4
    j = w % 4

    def wide_at(zz, jj):
        return zz * 4 + jj

    core_w = wide_at(z, j + 1 - 2 * (j % 2))
    side_w = wide_at(z, (j + 2) % 4)
    up_w = wide_at((z + 1) % 8, j)
    down_w = wide_at((z + 7) % 8, j)

    def xor8(a, v):
        out = 0
        for bit in range(3):
            p = 1 << bit
            ab = a // p % 2
            vb = v // p % 2
            out = out + p * ((ab + vb) % 2)
        return out

    pool_copy = pltpu.make_async_copy(pool_hbm, pool, pool_sem)
    pool_copy.start()

    barrier = pltpu.get_barrier_semaphore()
    quad_w = (w, core_w, side_w, wide_at(z, 3 - j))
    for ww in quad_w[1:] + (up_w, down_w):
        pl.semaphore_signal(barrier, inc=1, device_id={"req": r, "wide": ww}, device_id_type=MESH)
    for v in range(1, 8):
        pl.semaphore_signal(
            barrier, inc=1, device_id={"req": xor8(r, v), "wide": w}, device_id_type=MESH
        )
    pl.semaphore_wait(barrier, 12)

    copies = []

    def go(src, dst, ww):
        i = len(copies)
        copy = pltpu.make_async_remote_copy(
            src_ref=src, dst_ref=dst, send_sem=q_send.at[i], recv_sem=q_recv.at[i],
            device_id={"req": r, "wide": ww}, device_id_type=MESH,
        )
        copy.start()
        copies.append(copy)
        return copy

    def plane(src, dst, ssem, rsem, dest):
        return pltpu.make_async_remote_copy(
            src_ref=src, dst_ref=dst, send_sem=ssem, recv_sem=rsem,
            device_id={"req": dest, "wide": w}, device_id_type=MESH,
        )

    side = go(x_ref, xg.at[0, 1], side_w)
    up0 = go(x_ref, xg.at[1, 0], up_w)
    down0 = go(x_ref, xg.at[7, 0], down_w)
    core0 = go(x_ref, xg.at[0, 2], core_w)
    xg[0, 0] = x_ref[...]

    row8x = lax.broadcasted_iota(jnp.int32, (8, 512), 0)
    row8b = lax.broadcasted_iota(jnp.int32, (8, 128), 0)
    cbuf[15:16, :] = jnp.zeros((1, 256), F32)

    def fill_state(v):
        for i in range(2):
            slot = slot_ref[xor8(r, v) * 2 + i]
            mine = slot // 8 == r
            local = jnp.clip(slot - r * 8, 0, 7)
            sx[v, i * 192 : i * 192 + 192] = jnp.where(mine, pool[local, 0:192], 0.0).astype(BF)
            sy[v, i * YR : i * YR + YR] = jnp.where(mine, pool[local, 192:512], 0.0).astype(BF)
            for m in range(3):
                xrow = jnp.sum(jnp.where(row8x == slot - r * 8, cxp_ref[m].astype(F32), 0.0), 0, keepdims=True)
                brow = jnp.sum(jnp.where(row8b == slot - r * 8, cbp_ref[m].astype(F32), 0.0), 0, keepdims=True)
                e = i * 3 + m
                cbuf[2 * e : 2 * e + 1, :] = xrow[:, :256]
                cbuf[2 * e + 1 : 2 * e + 2, :] = xrow[:, 256:]
                cbuf[12 + e // 2 : 13 + e // 2, e % 2 * 128 : e % 2 * 128 + 128] = brow
        sx[v, 384:400] = cbuf[...].astype(BF)

    def sx_first(vy):
        return plane(sx.at[2 * vy + 1], sx1.at[vy], sx1_s.at[vy], sx1_r.at[vy], xor8(r, 1))

    def sy_first(vy):
        return plane(
            sy.at[pl.ds(2 * vy, 2)], sy1.at[vy], sy1_s.at[vy], sy1_r.at[vy], xor8(r, 2 * vy)
        )

    def sx_second(vy):
        return plane(sxs.at[vy], sx2.at[vy], sx2_s.at[vy], sx2_r.at[vy], xor8(r, 2 * vy))

    def sy_second():
        return plane(sys, sy2, sy2_s, sy2_r, xor8(r, 1))

    wbd_ref[:, :128] = wbc_ref[...]
    wide_dt = jnp.concatenate([wdt_ref[...].astype(F32), jnp.zeros((120, 1024), F32)], 0)
    wbd_ref[:, 128:] = wide_dt.T.astype(BF)

    side.wait_recv()
    up1 = go(xg.at[0, 1], xg.at[1, 1], up_w)
    down1 = go(xg.at[0, 1], xg.at[7, 1], down_w)
    core1 = go(xg.at[0, 1], xg.at[0, 3], core_w)
    pool_copy.wait()
    def via(n, src, dst):
        return plane(src, dst, via_s.at[n], via_r.at[n], xor8(r, 2 + 4 * (n % 2)))

    def sy_via(n):
        return via(n, sy.at[4 + n], via_sy.at[n])

    for vy in (2, 1, 3, 0):
        fill_state(2 * vy)
        fill_state(2 * vy + 1)
        if vy == 2:
            sy_via(0).start()
            sy_via(1).start()
        sx_first(vy).start()

    def state_join():
        for n, own, vy in ((0, 6, 3), (1, 3, 1)):
            sy_via(n).wait()
            sy[own] = sy[own] + via_sy[n]
            sy_first(vy).start()

    rows = [pl.multiple_of(xor8(j, q) * 256, 256) for q in ORDER]

    def compute(k):
        v = (z + 8 - k) % 8
        vy = v // 2
        vh = v % 2
        blocks = [xg[k, p] for p in range(4)]
        for part in range(3):
            def weights(p):
                if part < 2:
                    return wxz_ref[part, pl.ds(rows[p], 256), :]
                return wbd_ref[pl.ds(rows[p], 256), :]

            acc = jnp.dot(blocks[0], weights(0), preferred_element_type=F32)
            for p in range(1, 4):
                acc = acc + jnp.dot(blocks[p], weights(p), preferred_element_type=F32)
            if part == 0:
                py[v] = acc.astype(BF)
            elif part == 1:
                px[v, :, :512] = acc.astype(BF)
            else:
                px[v, :, 512:] = acc[:, :128].astype(BF)
                sdt[v] = acc[:, 128:].T[:8]

        @pl.when(v != 0)
        def _():
            plane(sdt.at[v], rdt.at[v], d_send.at[v], d_recv.at[v], xor8(r, v)).start()

        @pl.when(vh == 1)
        def _():
            plane(px.at[v], px1.at[vy], px1_s.at[vy], px1_r.at[vy], xor8(r, 1)).start()

        @pl.when(vy != 0)
        def _():
            plane(
                py.at[v], py1.at[v], py1_s.at[v], py1_r.at[v], xor8(r, vy * 2)
            ).start()

    def sx_via(n):
        part = slice(0, CUT) if n == 0 else slice(CUT, XR)
        return via(2 + n, sxs.at[2, part], via_sx.at[part])

    def state_second():
        sx_first(2).wait()
        sxs[2] = sx[4] + sx1[2]
        sx_via(0).start()
        sx_via(1).start()
        for vy in (1, 3):
            sx_first(vy).wait()
            sxs[vy] = sx[2 * vy] + sx1[vy]
        for vy in (1, 3):
            sy_first(vy).wait()
        sys[...] = (sy[1] + sy1[1, 1]) + sy1[3, 1]
        sy_second().start()

    def state_third():
        sx_via(0).wait()
        sxs[3, :CUT] = sxs[3, :CUT] + via_sx[:CUT]
        sx_second(3).start()
        sx_via(1).wait()
        sxs[1, CUT:] = sxs[1, CUT:] + via_sx[CUT:]
        sx_second(1).start()

    core0.wait_recv()
    core1.wait_recv()
    arrived = {(1, 0): up0, (1, 1): up1, (7, 0): down0, (7, 1): down1}
    for step in range(len(STEPS)):
        nxt = STEPS[step + 1] if step + 1 < len(STEPS) else ()
        partner = []

        def forward(p):
            for k in nxt:
                copy = arrived.pop((k, p), None)
                if copy is None:
                    continue
                copy.wait_recv()
                block = xg.at[k, p]
                if k in (1, 2) or (k == 3 and p == 0):
                    arrived[k + 1, p] = go(block, xg.at[k + 1, p], up_w)
                elif k in (7, 6) or (k == 5 and p == 1):
                    arrived[k - 1, p] = go(block, xg.at[k - 1, p], down_w)
                partner.append(go(block, xg.at[k, p + 2], core_w))

        forward(0)
        compute(STEPS[step][0])
        forward(1)
        for k in STEPS[step][1:]:
            compute(k)
        if step == 0:
            state_join()
        for copy in partner:
            copy.wait_recv()

    state_second()

    def px_first(vy):
        return plane(px.at[2 * vy + 1], px1.at[vy], px1_s.at[vy], px1_r.at[vy], xor8(r, 1))

    def py_first(v):
        return plane(py.at[v], py1.at[v], py1_s.at[v], py1_r.at[v], xor8(r, v // 2 * 2))

    def px_second(vy):
        return plane(pxs.at[vy], px2.at[vy], px2_s.at[vy], px2_r.at[vy], xor8(r, 2 * vy))

    def py_second():
        return plane(pys, py2, py2_s, py2_r, xor8(r, 1))

    def px_via(n):
        part = slice(128 * n, 128 * n + 128)
        return via(4 + n, pxs.at[2, part], via_px.at[part])

    px_first(2).wait()
    pxs[2] = (px[4].astype(F32) + px1[2].astype(F32)).astype(BF)
    px_via(0).start()
    px_via(1).start()
    state_third()
    for n, vy in ((0, 3), (1, 1)):
        px_first(vy).wait()
        px_via(n).wait()
        part = slice(128 * n, 128 * n + 128)
        rest = slice(128 - 128 * n, 256 - 128 * n)
        joined = px[2 * vy, part].astype(F32) + px1[vy, part].astype(F32) + via_px[part].astype(F32)
        pxs[vy, part] = joined.astype(BF)
        pxs[vy, rest] = (px[2 * vy, rest].astype(F32) + px1[vy, rest].astype(F32)).astype(BF)
        px_second(vy).start()
    for v in (3, 5, 7):
        py_first(v).wait()
    pys[...] = (
        (py[1].astype(F32) + py1[3].astype(F32)) + (py1[5].astype(F32) + py1[7].astype(F32))
    ).astype(BF)
    py_second().start()

    for copy in copies:
        copy.wait_send()
    for v in (2, 4, 6):
        py_first(v).wait()
    for v in range(1, 8):
        plane(sdt.at[v], rdt.at[v], d_send.at[v], d_recv.at[v], xor8(r, v)).wait()
    dts = sdt[0]
    for v in range(1, 8):
        dts = dts + rdt[v]

    start = start_ref[0, 1]
    live = [jnp.where(prefix_ref[i] > 0, 1.0, 0.0) for i in range(2)]

    head = lax.broadcasted_iota(jnp.int32, (8, 256), 0)
    lane = lax.broadcasted_iota(jnp.int32, (8, 256), 1)
    bias8 = jnp.zeros((8, 256), F32)
    rate8 = jnp.zeros((8, 256), F32)
    for h in range(8):
        bias8 = jnp.where(head == h, bias_ref[h], bias8)
        rate8 = jnp.where(head == h, rate_ref[h], rate8)
    raised = dts.astype(BF).astype(F32) + bias8
    step = jnp.maximum(raised, 0.0) + jnp.log1p(jnp.exp(-jnp.abs(raised)))
    rate = -jnp.exp(rate8) * step
    upper_s = lax.broadcasted_iota(jnp.int32, (256, 256), 0)
    upper_t = lax.broadcasted_iota(jnp.int32, (256, 256), 1)
    reach = jnp.where((upper_s <= upper_t) & ((upper_t < start) | (upper_s >= start)), 1.0, 0.0)
    top = rate.astype(BF).astype(F32)
    mid = (rate - top).astype(BF).astype(F32)
    low = rate - top - mid
    parts = jnp.concatenate([top, mid, low, jnp.zeros((8, 256), F32)], 0).astype(BF)
    sums = jnp.dot(parts, reach.astype(BF), preferred_element_type=F32)
    run = sums[0:8] + sums[8:16] + sums[16:24]
    late = lane >= start
    end = [
        jnp.sum(jnp.where(late, 0.0, rate), 1, keepdims=True),
        jnp.sum(jnp.where(late, rate, 0.0), 1, keepdims=True),
    ]
    to_end = jnp.exp(jnp.where(late, end[1], end[0]) - run) * step
    end_decay = [jnp.exp(end[0]), jnp.exp(end[1])]
    columns = jnp.concatenate([run, jnp.exp(run), jnp.zeros((112, 256), F32)], 0).T

    px_first(0).wait()
    sx_first(0).wait()
    for vy in (1, 3):
        sx_second(vy).wait()
        px_second(vy).wait()
    cbuf[...] = (
        (sx[0, 384:400] + sx1[0, 384:400]) + (sx2[1, 384:400] + sx2[3, 384:400])
    ).astype(F32)

    def total_x(c0, n):
        cols = slice(c0, c0 + n)
        out = px[0, :, cols].astype(F32) + px1[0, :, cols].astype(F32)
        for vy in (1, 3):
            out = out + px2[vy, :, cols].astype(F32)
        return out.astype(BF).astype(F32)

    def conv(values, taps, bias, cache):
        n = values.shape[1]
        tok = lax.broadcasted_iota(jnp.int32, (256, n), 0)
        out = bias + taps[3:4] * values
        for lag in range(1, 4):
            earlier = pltpu.roll(values, lag, 0)
            for i in range(2):
                for o in range(lag):
                    at = o if i == 0 else start + o
                    earlier = jnp.where(tok == at, cache(i, 3 + o - lag), earlier)
            out = out + taps[3 - lag : 4 - lag] * earlier
        return jax.nn.silu(out).astype(BF)

    def cache_b(i, m):
        e = i * 3 + m
        return cbuf[12 + e // 2 : 13 + e // 2, e % 2 * 128 : e % 2 * 128 + 128] * live[i]

    bcg[0] = conv(total_x(512, 128), cbw_ref[...], cbb_ref[...], cache_b)
    shares = []
    for q in range(1, 4):
        copy = pltpu.make_async_remote_copy(
            src_ref=bcg.at[0], dst_ref=bcg.at[q], send_sem=b_send.at[q], recv_sem=b_recv.at[q],
            device_id={"req": r, "wide": quad_w[q]}, device_id_type=MESH,
        )
        copy.start()
        shares.append(copy)

    for half in range(2):
        def cache_x(i, m):
            e = 2 * (i * 3 + m) + half
            return cbuf[e : e + 1, :] * live[i]

        cols = slice(half * 256, half * 256 + 256)
        xs = conv(total_x(half * 256, 256), cxw_ref[:, cols], cxb_ref[:, cols], cache_x)
        xsb[:, cols] = xs
        xst_ref[cols, :] = xs.astype(F32).T

    for copy in shares:
        copy.wait()

    def maps(a):
        ab = (a % 2 + j % 2) % 2 + 2 * ((a // 2 + j // 2) % 2)
        return bcg[ab]

    b_maps = jnp.concatenate([maps(0), maps(1)], 1)
    c_maps = jnp.concatenate([maps(2), maps(3)], 1)
    scores = lax.dot_general(
        c_maps, b_maps, (((1,), (1,)), ((), ())), preferred_element_type=F32
    )
    allowed = (upper_t <= upper_s) & ((upper_s < start) | (upper_t >= start))
    scores = jnp.where(allowed, scores, 0.0)
    first = lax.broadcasted_iota(jnp.int32, (256, 128), 1) < 64
    for pair in range(4):
        cols = slice(pair * 128, pair * 128 + 128)
        xs = xsb[:, cols]
        acc = None
        for side_h in range(2):
            h = 2 * pair + side_h
            gap = jnp.minimum(columns[:, h : h + 1] - run[h : h + 1, :], 0.0)
            weight = (jnp.exp(gap) * step[h : h + 1, :] * scores).astype(BF)
            kept = jnp.where(first == (side_h == 0), xs.astype(F32), 0.0).astype(BF)
            part = jnp.dot(weight, kept, preferred_element_type=F32)
            acc = part if acc is None else acc + part
        skip = jnp.where(first, skip_ref[2 * pair], skip_ref[2 * pair + 1])
        ybuf[:, cols] = acc + skip * xs.astype(F32)

    sy_second().wait()
    py_second().wait()

    def h0_piece(i, h):
        if h < 3:
            rows_h = slice(i * 192 + h * 64, i * 192 + h * 64 + 64)
            return (sx[0, rows_h] + sx1[0, rows_h]) + (sx2[1, rows_h] + sx2[3, rows_h])
        rows_h = slice(i * YR + (h - 3) * 64, i * YR + (h - 3) * 64 + 64)
        return (
            (sy[0, rows_h] + sy1[1, 0, rows_h]) + (sy1[3, 0, rows_h] + sy2[rows_h])
        )

    square = jnp.zeros((256, 128), F32)
    tok = lax.broadcasted_iota(jnp.int32, (256, 128), 0)
    h0 = [[None] * 8, [None] * 8]
    for pair in range(4):
        cols = slice(pair * 128, pair * 128 + 128)
        from_state = None
        for i in range(2):
            for h in (2 * pair, 2 * pair + 1):
                h0[i][h] = h0_piece(i, h)
            both = jnp.concatenate([h0[i][2 * pair], h0[i][2 * pair + 1]], 0)
            part = lax.dot_general(
                c_maps, both, (((1,), (1,)), ((), ())), preferred_element_type=F32
            ) * live[i]
            from_state = part if i == 0 else jnp.where(tok >= start, part, from_state)
        grown = jnp.where(
            first, columns[:, 8 + 2 * pair : 9 + 2 * pair], columns[:, 9 + 2 * pair : 10 + 2 * pair]
        )
        result = ybuf[:, cols] + from_state * grown
        gate = py[0, :, cols].astype(F32) + py2[:, cols].astype(F32)
        for v in (2, 4, 6):
            gate = gate + py1[v, :, cols].astype(F32)
        gated = result * jax.nn.silu(gate.astype(BF).astype(F32))
        ybuf[:, cols] = gated
        square = square + gated * gated

    ssq[0] = jnp.broadcast_to(jnp.sum(square.T, 0, keepdims=True), (8, 256))
    norms = []
    for q in range(1, 4):
        copy = pltpu.make_async_remote_copy(
            src_ref=ssq.at[0], dst_ref=ssq.at[q], send_sem=n_send.at[q], recv_sem=n_recv.at[q],
            device_id={"req": r, "wide": quad_w[q]}, device_id_type=MESH,
        )
        copy.start()
        norms.append(copy)

    for h in range(8):
        rows_h = slice(h * 64, h * 64 + 64)
        spread = xst_ref[rows_h, :] * to_end[h : h + 1, :]
        late_row = lax.broadcasted_iota(jnp.int32, (64, 256), 1) >= start
        for i in range(2):
            u = jnp.where(late_row == (i == 1), spread, 0.0).astype(BF)
            fresh = jnp.dot(u, b_maps, preferred_element_type=F32)
            keep = end_decay[i][h : h + 1, :] * live[i]
            state_out[i, rows_h, :] = keep * h0[i][h].astype(F32) + fresh

    for copy in norms:
        copy.wait()
    mean = (ssq[0] + ssq[1] + ssq[2] + ssq[3]) / (HEADS * HEAD_DIM // GROUPS)
    scale = jnp.broadcast_to(lax.rsqrt(mean + NORM_EPS)[0:1], (128, 256)).T
    for pair in range(4):
        cols = slice(pair * 128, pair * 128 + 128)
        y_out[:, cols] = (ybuf[:, cols] * scale * gain_ref[:, cols]).astype(BF)


def project(*args):
    vm = pl.BlockSpec(memory_space=pltpu.VMEM)
    sm = pl.BlockSpec(memory_space=pltpu.SMEM)
    dma = pltpu.SemaphoreType.DMA
    n_q = 3 + 14 + 14 + 2
    return pl.pallas_call(
        project_kernel,
        out_shape=(
            jax.ShapeDtypeStruct((256, 512), BF),
            jax.ShapeDtypeStruct((2, 512, 256), F32),
        ),
        in_specs=[vm] * 4 + [sm] * 6 + [vm] * 7 + [pl.BlockSpec(memory_space=pl.ANY)],
        out_specs=(vm,) * 2,
        scratch_shapes=[
            pltpu.VMEM((1024, 256), BF),
            pltpu.VMEM((16, 256), F32),
            pltpu.VMEM((256, 512), BF),
            pltpu.VMEM((512, 256), F32),
            pltpu.VMEM((256, 512), F32),
            pltpu.VMEM((4, 256, 128), BF),
            pltpu.VMEM((4, 8, 256), F32),
            dma((4,)), dma((4,)), dma((4,)), dma((4,)),
            pltpu.VMEM((2, 2 * YR, 256), BF),
            pltpu.VMEM((XR, 256), BF),
            pltpu.VMEM((256, XC), BF),
            dma((6,)), dma((6,)),
            pltpu.VMEM((8, 4, 256, 256), BF),
            pltpu.VMEM((8, 256, XC), BF),
            pltpu.VMEM((4, 256, XC), BF),
            pltpu.VMEM((4, 256, XC), BF),
            pltpu.VMEM((4, 256, XC), BF),
            pltpu.VMEM((8, 256, YC), BF),
            pltpu.VMEM((8, 256, YC), BF),
            pltpu.VMEM((256, YC), BF),
            pltpu.VMEM((256, YC), BF),
            pltpu.VMEM((8, 8, 256), F32),
            pltpu.VMEM((8, 8, 256), F32),
            pltpu.VMEM((8, 512, 256), F32),
            pltpu.VMEM((8, XR, 256), BF),
            pltpu.VMEM((4, XR, 256), BF),
            pltpu.VMEM((4, XR, 256), BF),
            pltpu.VMEM((4, XR, 256), BF),
            pltpu.VMEM((8, 2 * YR, 256), BF),
            pltpu.VMEM((4, 2, 2 * YR, 256), BF),
            pltpu.VMEM((2 * YR, 256), BF),
            pltpu.VMEM((2 * YR, 256), BF),
            dma(()),
            dma((n_q,)), dma((n_q,)), dma((8,)), dma((8,)),
            dma((4,)), dma((4,)), dma((4,)), dma((4,)), dma((8,)), dma((8,)), dma(()), dma(()),
            dma((4,)), dma((4,)), dma((4,)), dma((4,)), dma((4,)), dma((4,)), dma(()), dma(()),
        ],
        compiler_params=pltpu.CompilerParams(
            collective_id=0, has_side_effects=True, vmem_limit_bytes=56 << 20
        ),
        name="project",
    )(*args)


def on_device(
    x_in, w_xz, w_dt, w_bc, dt_bias, a_log, d_skip, conv_x_w, conv_x_b, conv_bc_w, conv_bc_b,
    norm_gain, stretch_start, prefix_len, state_slot, ssm_pool, conv_x_pool, conv_bc_pool,
):
    route = []
    for r in range(8):
        for w in range(32):
            f, j = w // 4, w % 4
            route.append((w * 8 + r, ((r ^ f) * 4 + j) * 8 + f))
    x_t = lax.ppermute(x_in, ("wide", "req"), route)
    y, state = project(
        x_t, jnp.transpose(w_xz, (1, 0, 2)), w_bc, w_dt.T,
        state_slot, stretch_start, prefix_len, dt_bias, a_log, d_skip,
        conv_x_w, conv_x_b[None], conv_bc_w, conv_bc_b[None], norm_gain[None],
        jnp.transpose(conv_x_pool, (1, 0, 2)), jnp.transpose(conv_bc_pool, (1, 0, 2)),
        ssm_pool.reshape(8, 512, 256),
    )
    return y, state.reshape(2, 8, 64, 256)


def solution(mesh):
    in_specs = (
        P("req", "wide"), P("req", None, "wide"), P("req", "wide"), P("req", "wide"),
        P("wide"), P("wide"), P("wide"), P(None, "wide"), P("wide"), P(None, "wide"),
        P("wide"), P("wide"), P("req", None), P("req"), P(),
        P("req", "wide", None, None), P("req", None, "wide"), P("req", None, "wide"),
    )
    out_specs = (P("req", "wide"), P("req", "wide", None, None))
    return jax.shard_map(
        on_device, mesh=mesh, in_specs=in_specs, out_specs=out_specs, check_vma=False
    )
```
